256 devices in a mesh: row: 16 (over x, y), col: 16 (over z, core).
Axes of the slice: x: 4, y: 4, z: 8, core: 2. Of those that a mesh axis runs over, the one named last changes fastest.
Arguments:
- fixed_section: bfloat16 [512, 2048], P('row', 'col'), may hold values from -6 to 6
- moving_section: bfloat16 [512, 2048], P('row', 'col'), may hold values from -6 to 6
- field_init: float32 [2, 512, 2048], P(None, 'row', 'col'), may hold values from -48 to 48
- first_weight: float32 [8, 9], replicated, may hold values from -2 to 2
- first_bias: float32 [8], replicated, may hold values from -0.5 to 0.5
- second_weight: float32 [8, 8, 9], replicated, may hold values from -0.75 to 0.75
Outputs:
- field_change: float32 [2, 512, 2048], P(None, 'row', 'col')
The draws below stay inside these ranges and needn't reach their ends.
All inputs are finite; a program needn't handle non-finite values.
Results may differ from the reference program's by a relative error of at most 0.011.
Values may be sent and summed in bfloat16 or wider, within the bound.
A program may use at most 64 MiB of HBM per device.

```python
import jax
import jax.numpy as jnp
from jax import lax

CH = 8
REACH = 16
ITERS = 3
H = 512
W = 2048


def shard_levels(own_key, dims, pieces, least, high):
    def one(axis_at, parts):
        heights = jax.random.uniform(jax.random.fold_in(jax.random.fold_in(own_key, 6), axis_at), (parts,), jnp.float32, least / len(pieces), high / len(pieces))
        return jnp.repeat(jnp.exp(heights), dims[axis_at] // parts).reshape((-1,) + (1,) * (len(dims) - axis_at - 1))

    factor_of = one(*pieces[0])
    for cut in pieces[1:]:
        factor_of = factor_of * one(*cut)
    return factor_of


def scatter_about(stream_key, dims, width, most, pieces=(), held_as=jnp.bfloat16):
    drawn = jax.random.normal(stream_key, dims, jnp.float32) * width
    if len(pieces) > 0:
        drawn = shard_levels(stream_key, dims, pieces, -0.22, 0.18) * drawn
    return jnp.clip(drawn, min=-most, max=most).astype(held_as)


def setup_inputs(seed: int = 0) -> dict:
    seeds = jax.random.split(jax.random.key(seed), 7)
    return {
        "fixed_section": scatter_about(seeds[0], (H, W), 1.0, 6.0, ((0, 16), (1, 16))),
        "moving_section": scatter_about(seeds[1], (H, W), 1.0, 6.0, ((0, 16), (1, 16))),
        "field_init": scatter_about(seeds[2], (2, H, W), REACH, 48.0, ((1, 16), (2, 16)), jnp.float32),
        "first_weight": scatter_about(seeds[3], (CH, 9), 9 ** -0.5, 2.0, (), jnp.float32),
        "first_bias": jnp.clip(jax.random.uniform(seeds[4], (CH,), jnp.float32, -0.5, 0.5), -0.5, 0.5),
        "second_weight": scatter_about(seeds[5], (CH, CH, 9), (9 * CH) ** -0.5, 0.75, (), jnp.float32),
    }


stiffness = 0.01
step_size = 0.5
adam_epsilon = 0.01

def encode(image_ext, first_weight, first_bias, second_weight, first_mask):
    out_rows = image_ext.shape[0] - 2
    out_cols = image_ext.shape[1] - 2
    hidden = jnp.zeros((first_weight.shape[0], out_rows, out_cols), jnp.float32) + first_bias[:, None, None]
    for tap_index in range(9):
        tap_row = tap_index // 3
        tap_col = tap_index % 3
        hidden = hidden + first_weight[:, tap_index, None, None] * image_ext[None, tap_row:tap_row + out_rows, tap_col:tap_col + out_cols]
    hidden = jnp.maximum(hidden, 0.0) * first_mask
    out_rows = out_rows - 2
    out_cols = out_cols - 2
    embedding = jnp.zeros((second_weight.shape[0], out_rows, out_cols), jnp.float32)
    for tap_index in range(9):
        tap_row = tap_index // 3
        tap_col = tap_index % 3
        embedding = embedding + jnp.einsum('oc,chw->ohw', second_weight[:, :, tap_index], hidden[:, tap_row:tap_row + out_rows, tap_col:tap_col + out_cols], precision=lax.Precision.HIGHEST)
    return embedding

def sample(flattened, ext_cols, displace, margin, fixed_embedding):
    channels = fixed_embedding.shape[0]
    out_rows = displace.shape[1]
    out_cols = displace.shape[2]
    nearest = jnp.floor(displace + 0.5)
    fraction = displace - nearest
    offsets = nearest.astype(jnp.int32)
    spline = [0.5 * (0.5 - fraction) ** 2, 0.75 - fraction * fraction, 0.5 * (0.5 + fraction) ** 2]
    slopes = [fraction - 0.5, -2.0 * fraction, 0.5 + fraction]
    base_row = lax.broadcasted_iota(jnp.int32, (out_rows, out_cols), 0) + margin + offsets[0]
    base_col = lax.broadcasted_iota(jnp.int32, (out_rows, out_cols), 1) + margin + offsets[1]
    warped = jnp.zeros((channels, out_rows, out_cols), jnp.float32)
    along_row = jnp.zeros((channels, out_rows, out_cols), jnp.float32)
    along_col = jnp.zeros((channels, out_rows, out_cols), jnp.float32)
    for tap_row in range(3):
        for tap_col in range(3):
            position = (base_row + (tap_row - 1)) * ext_cols + base_col + (tap_col - 1)
            picked = jnp.take(flattened, position.reshape(-1), axis=1).reshape(channels, out_rows, out_cols)
            warped = warped + (spline[tap_row][0] * spline[tap_col][1])[None] * picked
            along_row = along_row + (slopes[tap_row][0] * spline[tap_col][1])[None] * picked
            along_col = along_col + (spline[tap_row][0] * slopes[tap_col][1])[None] * picked
    mismatch = warped - fixed_embedding
    factor = 2.0 / channels
    return jnp.stack([lax.optimization_barrier(jnp.sum(mismatch * along_row, axis=0)) * factor, lax.optimization_barrier(jnp.sum(mismatch * along_col, axis=0)) * factor])

def reference(fixed_section, moving_section, field_init, first_weight, first_bias, second_weight):
    full_rows, full_cols = fixed_section.shape
    margin = REACH + 1
    mask_rows = lax.broadcasted_iota(jnp.int32, (full_rows + 2, full_cols + 2), 0) - 1
    mask_cols = lax.broadcasted_iota(jnp.int32, (full_rows + 2, full_cols + 2), 1) - 1
    first_mask = ((mask_rows >= 0) & (mask_rows < full_rows) & (mask_cols >= 0) & (mask_cols < full_cols)).astype(jnp.float32)
    fixed_embedding = encode(jnp.pad(fixed_section.astype(jnp.float32), 2), first_weight, first_bias, second_weight, first_mask)
    moving_embedding = encode(jnp.pad(moving_section.astype(jnp.float32), 2), first_weight, first_bias, second_weight, first_mask)
    padded_moving = jnp.pad(moving_embedding, ((0, 0), (margin, margin), (margin, margin)))
    channels, ext_rows, ext_cols = padded_moving.shape
    flattened = padded_moving.reshape(channels, ext_rows * ext_cols)
    raw_field = field_init
    first_moment = jnp.zeros_like(field_init)
    second_moment = jnp.zeros_like(field_init)
    for iteration in range(ITERS):
        squashed = jnp.tanh(raw_field / REACH)
        displace = REACH * squashed
        data_term = sample(flattened, ext_cols, displace, margin, fixed_embedding)
        padded = jnp.pad(displace, ((0, 0), (1, 1), (1, 1)))
        neighbours = padded[:, 2:, 1:-1] + padded[:, :-2, 1:-1] + padded[:, 1:-1, 2:] + padded[:, 1:-1, :-2]
        gradient = (data_term + 2.0 * stiffness * (4.0 * displace - neighbours)) * (1.0 - squashed * squashed)
        first_moment = 0.9 * first_moment + 0.1 * gradient
        second_moment = 0.999 * second_moment + 0.001 * gradient * gradient
        corrected_one = first_moment / (1.0 - 0.9 ** (iteration + 1))
        corrected_two = second_moment / (1.0 - 0.999 ** (iteration + 1))
        raw_field = raw_field - step_size * corrected_one / (jnp.sqrt(corrected_two) + adam_epsilon)
    return raw_field - field_init
```

```python
import functools

import jax
import jax.numpy as jnp
from jax import lax
from jax.experimental import pallas as pl
from jax.experimental.pallas import tpu as pltpu
from jax.sharding import PartitionSpec as P

REACH = 16
ITERS = 3
CH = 8

stiffness = 0.01
step_size = 0.5
adam_epsilon = 0.01

F32 = jnp.float32
BF16 = jnp.bfloat16
MESH = pl.DeviceIdType.MESH
AROUND = [(i, j) for i in (-1, 0, 1) for j in (-1, 0, 1) if (i, j) != (0, 0)]
SIDES = [(-1, 0), (1, 0), (0, -1), (0, 1)]
SLAB = 14


def lanes(shape):
    return lax.broadcasted_iota(jnp.int32, shape, len(shape) - 1)


def split(x):
    high = x.astype(BF16)
    return high, (x - high.astype(F32)).astype(BF16)


def dot(a, b):
    return lax.dot_general(a, b, (((1,), (0,)), ((), ())), preferred_element_type=F32)


def kernel(
    rows_of_mesh,
    cols_of_mesh,
    fixed_ref,
    moving_ref,
    field_ref,
    w1_ref,
    b1_ref,
    w2_ref,
    out_ref,
    own,
    around,
    shifted,
    toeplitz,
    lhs,
    fixed_embed,
    disp,
    edge_row,
    edge_col,
    raw,
    first_moment,
    second_moment,
    weights,
    data,
    image_send,
    image_recv,
    disp_send,
    disp_recv,
):
    me_row, me_col = lax.axis_index("row"), lax.axis_index("col")
    tile_rows, tile_cols = fixed_ref.shape

    def at(offset):
        i, j = offset
        return (
            lax.rem(me_row + (i + rows_of_mesh), rows_of_mesh),
            lax.rem(me_col + (j + cols_of_mesh), cols_of_mesh),
        )

    barrier = pltpu.get_barrier_semaphore()
    for offset in AROUND:
        pl.semaphore_signal(barrier, inc=1, device_id=at(offset), device_id_type=MESH)

    own[0] = fixed_ref[...]
    own[1] = moving_ref[...]
    raw[...] = field_ref[...]
    first_moment[...] = jnp.zeros_like(first_moment)
    second_moment[...] = jnp.zeros_like(second_moment)
    disp[0] = REACH * jnp.tanh(field_ref[...] / REACH)

    def image_copy(offset):
        i, j = offset
        slot = 3 * (1 - i) + 1 - j
        return pltpu.make_async_remote_copy(
            src_ref=own,
            dst_ref=around.at[slot],
            send_sem=image_send.at[slot],
            recv_sem=image_recv.at[slot],
            device_id=at(offset),
            device_id_type=MESH,
        )

    def disp_copy(step, side):
        i, j = SIDES[side]
        if side == 0:
            src, dst = disp.at[step, :, pl.ds(tile_rows - 8, 8), :], edge_row.at[step, 0]
        elif side == 1:
            src, dst = disp.at[step, :, pl.ds(0, 8), :], edge_row.at[step, 1]
        else:
            src, dst = disp.at[step], edge_col.at[step, side - 2]
        return pltpu.make_async_remote_copy(
            src_ref=src,
            dst_ref=dst,
            send_sem=disp_send.at[step, side],
            recv_sem=disp_recv.at[step, side],
            device_id=at((-i, -j)),
            device_id_type=MESH,
        )

    pl.semaphore_wait(barrier, len(AROUND))
    for offset in AROUND:
        image_copy(offset).start()
    for side in range(4):
        disp_copy(0, side).start()

    sub64 = lax.broadcasted_iota(jnp.int32, (64, 128), 0)
    lane64 = lanes((64, 128))
    w2 = w2_ref[...].reshape(64, 9)
    for tap_col in range(3):
        spread = jnp.zeros((64, 128), F32)
        for tap_row in range(3):
            column = w2[:, 3 * tap_row + tap_col : 3 * tap_row + tap_col + 1]
            spread = jnp.where(
                lane64 == tap_row * 8 + (sub64 & 7), jnp.broadcast_to(column, (64, 128)), spread
            )
        base = jnp.sum(spread.reshape(8, 8, 128), axis=1)
        block = jnp.concatenate(
            [base if i == 0 else pltpu.roll(base, 8 * i, 1) for i in range(SLAB)], axis=0
        )
        high, low = split(block)
        at_row = tap_col * SLAB * 8
        toeplitz[at_row : at_row + SLAB * 8, 0:128] = high
        toeplitz[at_row : at_row + SLAB * 8, 128:256] = low
    w1 = w1_ref[...]
    taps = [jnp.broadcast_to(w1[:, k : k + 1], (8, 256)) for k in range(9)]
    sub8 = lax.broadcasted_iota(jnp.int32, (8, 256), 0)
    bias = jnp.zeros((8, 256), F32)
    for ch in range(CH):
        bias = jnp.where(sub8 == ch, b1_ref[ch], bias)

    for offset in AROUND:
        image_copy(offset).wait()

    full_rows, full_cols = rows_of_mesh * tile_rows, cols_of_mesh * tile_cols
    lane_tile = lanes((80, 128))

    def encode(which, first_lane, first_row, margin, slabs, store):
        def tile(slot):
            if slot == 4:
                return own[which].astype(F32)
            row, col = me_row + (slot // 3 - 1), me_col + (slot % 3 - 1)
            inside = (row >= 0) & (row < rows_of_mesh) & (col >= 0) & (col < cols_of_mesh)
            return around[slot, which].astype(F32) * jnp.where(inside, 1.0, 0.0).astype(F32)

        bands = []
        for col in range(3):
            bands.append(
                jnp.concatenate(
                    [tile(col)[8:, :], tile(3 + col), tile(6 + col)[: tile_rows - 8, :]], axis=0
                )
            )
        for tap_col in range(3):
            start = first_lane + tap_col
            if start == 128:
                left, right = bands[1], bands[2]
            else:
                turned = [pltpu.roll(x, 128 - start, 1) for x in bands]
                inside = lane_tile < 128 - start
                left = jnp.where(inside, turned[0], turned[1])
                right = jnp.where(inside, turned[1], turned[2])
            shifted[tap_col, :, 0:128] = left
            shifted[tap_col, :, 128:256] = right

        lane8 = lanes((8, 256))
        col8 = me_col * tile_cols + lane8 - (margin + 1)
        col_in = (col8 >= 0) & (col8 < full_cols)
        lane_e = lanes((SLAB * 8, 256))
        row_e = lax.broadcasted_iota(jnp.int32, (SLAB * 8, 256), 0) // 8
        col_e = me_col * tile_cols + lane_e - margin
        ok_col = (col_e >= 0) & (col_e < full_cols) & (lane_e < tile_cols + 2 * margin)

        for slab in slabs:
            hidden = []
            for i in range(SLAB + 2):
                h = bias
                for tap in range(9):
                    pixel = shifted[tap % 3, pl.ds(first_row + slab + i + tap // 3, 1), :]
                    h = h + taps[tap] * jnp.broadcast_to(pixel, (8, 256))
                row = me_row * tile_rows + (slab + i - margin - 1)
                row_ok = (row >= 0) & (row < full_rows)
                row_factor = jnp.where(row_ok, 1.0, 0.0).astype(F32)
                hidden.append(jnp.where(col_in, jnp.maximum(h, 0.0) * row_factor, 0.0))
            high, low = split(jnp.concatenate(hidden, axis=0))
            t_high, t_low = toeplitz[:, 0:128], toeplitz[:, 128:256]
            product = dot(
                jnp.concatenate([t_high, t_high], axis=1), jnp.concatenate([high, low], axis=0)
            ) + dot(t_low, high)
            n = SLAB * 8
            embed = (
                product[0:n]
                + pltpu.roll(product[n : 2 * n], 255, 1)
                + pltpu.roll(product[2 * n : 3 * n], 254, 1)
            )
            row_abs = me_row * tile_rows + row_e + (slab - margin)
            embed = jnp.where(ok_col & (row_abs >= 0) & (row_abs < full_rows), embed, 0.0)
            store(slab, embed)

    def halves(even, odd, low_half):
        axis = even.ndim - 1
        return (
            jnp.where(low_half, even, pltpu.roll(odd, 64, axis)),
            jnp.where(low_half, pltpu.roll(even, 64, axis), odd),
        )

    low8 = lanes((8, 128)) < 64

    def store_fixed(slab, embed):
        for pair in range(SLAB // 2):
            even = embed[pair * 16 : pair * 16 + 8, 0:128]
            odd = embed[pair * 16 + 8 : pair * 16 + 16, 0:128]
            left, right = halves(even, odd, low8)
            fixed_embed[slab // 2 + pair] = left
            fixed_embed[16 + slab // 2 + pair] = right

    low_e = lanes((SLAB * 8, 128)) < 64

    def store_moving(slab, embed):
        a, b = embed[:, 0:128], embed[:, 128:256]
        middle = jnp.where(low_e, pltpu.roll(a, 64, 1), pltpu.roll(b, 64, 1))
        for half, part in enumerate((a, middle)):
            high, low = split(part)
            lhs[half, slab * 8 : (slab + SLAB) * 8, 0:128] = high
            lhs[half, slab * 8 : (slab + SLAB) * 8, 128:256] = low

    encode(0, 126, 22, 0, (0, 14, 18), store_fixed)
    encode(1, 109, 5, REACH + 1, (0, 14, 28, 42, 52), store_moving)

    low16 = lanes((16, 128)) < 64
    lane32 = lanes((32, 128))
    position = (lane32 & 63).astype(F32) + (REACH + 1)
    second_row = jnp.where(lane32 >= 64, 1.0, 0.0).astype(F32)
    row32 = lax.broadcasted_iota(jnp.int32, (tile_rows, tile_cols), 0)
    has_north = jnp.where(me_row > 0, 1.0, 0.0).astype(F32)
    has_south = jnp.where(me_row < rows_of_mesh - 1, 1.0, 0.0).astype(F32)
    has_west = jnp.where(me_col > 0, 1.0, 0.0).astype(F32)
    has_east = jnp.where(me_col < cols_of_mesh - 1, 1.0, 0.0).astype(F32)

    def step(it, carry):
        grouped = []
        for comp in range(2):
            even = disp[it, comp, pl.ds(0, 16, stride=2), :]
            odd = disp[it, comp, pl.ds(1, 16, stride=2), :]
            grouped.append(jnp.concatenate(halves(even, odd, low16), axis=0))
        for comp in range(2):
            nearest = jnp.floor(grouped[comp] + 0.5)
            f = grouped[comp] - nearest
            at_w = 6 * comp
            weights[at_w] = 0.5 * (0.5 - f) * (0.5 - f)
            weights[at_w + 1] = 0.75 - f * f
            weights[at_w + 2] = 0.5 * (0.5 + f) * (0.5 + f)
            weights[at_w + 3] = f - 0.5
            weights[at_w + 4] = -2.0 * f
            weights[at_w + 5] = 0.5 + f
            if comp == 0:
                weights[12] = nearest + REACH + second_row
            else:
                weights[13] = nearest + position

        place = lax.broadcasted_iota(jnp.int32, (128, 128), 0).astype(F32)

        def sample(index, carry):
            half = index // 8
            quad = lax.rem(index, 8)
            columns = []
            for j in range(2):
                group = half * 16 + quad * 2 + j
                target = jnp.broadcast_to(weights[13, pl.ds(group, 1), :], (128, 128))
                off = place - target
                for b in range(3):
                    columns.append(jnp.where(off == b - 1, 1.0, 0.0).astype(BF16))
            onehot = jnp.concatenate(columns, axis=1)
            window = lhs[half, pl.ds(pl.multiple_of(quad * 32, 32), 304), :]
            picked = dot(window, jnp.concatenate([onehot, onehot], axis=0))
            for j in range(2):
                group = half * 16 + quad * 2 + j

                def weight(k):
                    return jnp.broadcast_to(weights[k, pl.ds(group, 1), :], (8, 128))

                offset = weight(12)
                masks = []
                for shift in (17, 8, 4, 2, 1, 1):
                    mask = offset >= shift
                    masks.append(mask)
                    offset = jnp.where(mask, offset - shift, offset)
                taps_at = []
                for b in range(3):
                    n = 3 * j + b
                    rows = [
                        picked[(2 * j + k) * 8 : (2 * j + k) * 8 + 8, n * 128 : n * 128 + 128]
                        for k in range(36)
                    ]
                    for shift, mask, count in zip(
                        (17, 8, 4, 2, 1, 1), masks, (19, 11, 7, 5, 4, 3)
                    ):
                        rows = [jnp.where(mask, rows[k + shift], rows[k]) for k in range(count)]
                    taps_at.append(rows)
                warped = slope_row = slope_col = None
                for b in range(3):
                    along = sum(weight(a) * taps_at[b][a] for a in range(3))
                    slant = sum(weight(3 + a) * taps_at[b][a] for a in range(3))
                    w, dw = weight(6 + b), weight(9 + b)
                    terms = (w * along, w * slant, dw * along)
                    if b == 0:
                        warped, slope_row, slope_col = terms
                    else:
                        warped += terms[0]
                        slope_row += terms[1]
                        slope_col += terms[2]
                mismatch = warped - fixed_embed[group]
                data[0, pl.ds(group, 1), :] = jnp.sum(mismatch * slope_row, axis=0, keepdims=True)
                data[1, pl.ds(group, 1), :] = jnp.sum(mismatch * slope_col, axis=0, keepdims=True)
            return carry

        lax.fori_loop(0, 16, sample, 0)

        for side in range(4):
            disp_copy(it, side).wait_recv()
        lane = lanes((tile_rows, tile_cols))
        one = jnp.where(it == 0, 1 / (1 - 0.9), jnp.where(it == 1, 1 / (1 - 0.9**2), 1 / (1 - 0.9**3)))
        two = jnp.where(
            it == 0, 1 / (1 - 0.999), jnp.where(it == 1, 1 / (1 - 0.999**2), 1 / (1 - 0.999**3))
        )
        for comp in range(2):
            even, odd = halves(data[comp, 0:16, :], data[comp, 16:32, :], low16)
            out_ref[comp, pl.ds(0, 16, stride=2), :] = even
            out_ref[comp, pl.ds(1, 16, stride=2), :] = odd
            sampled = out_ref[comp] * (2.0 / CH)
            d = disp[it, comp]
            north = jnp.where(
                row32 == 0, has_north * edge_row[it, 0, comp, 7:8, :], pltpu.roll(d, 1, 0)
            )
            south = jnp.where(
                row32 == tile_rows - 1,
                has_south * edge_row[it, 1, comp, 0:1, :],
                pltpu.roll(d, tile_rows - 1, 0),
            )
            west = pltpu.roll(
                jnp.where(lane == tile_cols - 1, has_west * edge_col[it, 0, comp], d), 1, 1
            )
            east = pltpu.roll(
                jnp.where(lane == 0, has_east * edge_col[it, 1, comp], d), tile_cols - 1, 1
            )
            squashed = d * (1.0 / REACH)
            gradient = (
                sampled + 2.0 * stiffness * (4.0 * d - (south + north + east + west))
            ) * (1.0 - squashed * squashed)
            m1 = 0.9 * first_moment[comp] + 0.1 * gradient
            m2 = 0.999 * second_moment[comp] + 0.001 * gradient * gradient
            first_moment[comp] = m1
            second_moment[comp] = m2
            new = raw[comp] - step_size * (m1 * one) / (jnp.sqrt(m2 * two) + adam_epsilon)
            raw[comp] = new

            @pl.when(it < ITERS - 1)
            def _():
                disp[it + 1, comp] = REACH * jnp.tanh(new / REACH)

        @pl.when(it < ITERS - 1)
        def _():
            for side in range(4):
                disp_copy(it + 1, side).start()

        return carry

    lax.fori_loop(0, ITERS, step, 0)
    out_ref[...] = raw[...] - field_ref[...]
    for it in range(ITERS):
        for side in range(4):
            disp_copy(it, side).wait_send()


def local(rows_of_mesh, cols_of_mesh, fixed, moving, field, w1, b1, w2):
    tile_rows, tile_cols = fixed.shape
    vmem = pl.BlockSpec(memory_space=pltpu.VMEM)
    tile = (tile_rows, tile_cols)
    return pl.pallas_call(
        functools.partial(kernel, rows_of_mesh, cols_of_mesh),
        out_shape=jax.ShapeDtypeStruct(field.shape, F32),
        in_specs=[vmem, vmem, vmem, vmem, pl.BlockSpec(memory_space=pltpu.SMEM), vmem],
        out_specs=vmem,
        scratch_shapes=[
            pltpu.VMEM((2,) + tile, BF16),
            pltpu.VMEM((9, 2) + tile, BF16),
            pltpu.VMEM((3, 80, 256), F32),
            pltpu.VMEM((3 * SLAB * 8, 256), BF16),
            pltpu.VMEM((2, 66 * 8, 256), BF16),
            pltpu.VMEM((32, 8, 128), F32),
            pltpu.VMEM((ITERS, 2) + tile, F32),
            pltpu.VMEM((ITERS, 2, 2, 8, tile_cols), F32),
            pltpu.VMEM((ITERS, 2, 2) + tile, F32),
            pltpu.VMEM((2,) + tile, F32),
            pltpu.VMEM((2,) + tile, F32),
            pltpu.VMEM((2,) + tile, F32),
            pltpu.VMEM((14, 32, 128), F32),
            pltpu.VMEM((2, 32, 128), F32),
            pltpu.SemaphoreType.DMA((9,)),
            pltpu.SemaphoreType.DMA((9,)),
            pltpu.SemaphoreType.DMA((ITERS, 4)),
            pltpu.SemaphoreType.DMA((ITERS, 4)),
        ],
        compiler_params=pltpu.CompilerParams(
            collective_id=0, has_side_effects=True, vmem_limit_bytes=40 << 20
        ),
        name="refine",
    )(fixed, moving, field, w1, b1, w2)


def solution(mesh):
    return jax.shard_map(
        functools.partial(local, mesh.shape["row"], mesh.shape["col"]),
        mesh=mesh,
        in_specs=(P("row", "col"), P("row", "col"), P(None, "row", "col"), P(), P(), P()),
        out_specs=P(None, "row", "col"),
        check_vma=False,
    )
```

```python
import functools

import jax
import jax.numpy as jnp
from jax import lax
from jax.experimental import pallas as pl
from jax.experimental.pallas import tpu as pltpu
from jax.sharding import PartitionSpec as P

REACH = 16
ITERS = 3
CH = 8

stiffness = 0.01
step_size = 0.5
adam_epsilon = 0.01

F32 = jnp.float32
BF16 = jnp.bfloat16
MESH = pl.DeviceIdType.MESH
AROUND = [(i, j) for i in (-1, 0, 1) for j in (-1, 0, 1) if (i, j) != (0, 0)]
SIDES = [(-1, 0), (1, 0), (0, -1), (0, 1)]
SLAB = 14


def lanes(shape):
    return lax.broadcasted_iota(jnp.int32, shape, len(shape) - 1)


def split(x):
    high = x.astype(BF16)
    return high, (x - high.astype(F32)).astype(BF16)


def dot(a, b):
    return lax.dot_general(a, b, (((1,), (0,)), ((), ())), preferred_element_type=F32)


def kernel(
    rows_of_mesh,
    cols_of_mesh,
    fixed_hbm,
    moving_hbm,
    field_hbm,
    w1_hbm,
    b1_hbm,
    w2_hbm,
    out_ref,
    field_ref,
    w1_ref,
    b1_ref,
    w2_ref,
    own,
    around,
    shifted,
    toeplitz,
    lhs,
    fixed_embed,
    disp,
    edge_row,
    edge_col,
    raw,
    first_moment,
    second_moment,
    weights,
    data,
    image_send,
    image_recv,
    disp_send,
    disp_recv,
    load_sem,
):
    me_row, me_col = lax.axis_index("row"), lax.axis_index("col")
    tile_rows, tile_cols = fixed_hbm.shape

    def at(offset):
        i, j = offset
        return (
            lax.rem(me_row + (i + rows_of_mesh), rows_of_mesh),
            lax.rem(me_col + (j + cols_of_mesh), cols_of_mesh),
        )

    barrier = pltpu.get_barrier_semaphore()
    for offset in AROUND:
        pl.semaphore_signal(barrier, inc=1, device_id=at(offset), device_id_type=MESH)

    loads = [
        pltpu.make_async_copy(src, dst, load_sem.at[i])
        for i, (src, dst) in enumerate(
            [
                (field_hbm, field_ref),
                (moving_hbm, own.at[1]),
                (fixed_hbm, own.at[0]),
                (w2_hbm, w2_ref),
                (w1_hbm, w1_ref),
                (b1_hbm, b1_ref),
            ]
        )
    ]
    for load in loads:
        load.start()
    first_moment[...] = jnp.zeros_like(first_moment)
    second_moment[...] = jnp.zeros_like(second_moment)
    loads[0].wait()
    raw[...] = field_ref[...]
    disp[0] = REACH * jnp.tanh(field_ref[...] / REACH)
    for load in loads[1:]:
        load.wait()

    def image_copy(offset):
        i, j = offset
        slot = 3 * (1 - i) + 1 - j
        return pltpu.make_async_remote_copy(
            src_ref=own,
            dst_ref=around.at[slot],
            send_sem=image_send.at[slot],
            recv_sem=image_recv.at[slot],
            device_id=at(offset),
            device_id_type=MESH,
        )

    def disp_copy(step, side):
        i, j = SIDES[side]
        if side == 0:
            src, dst = disp.at[step, :, pl.ds(tile_rows - 8, 8), :], edge_row.at[step, 0]
        elif side == 1:
            src, dst = disp.at[step, :, pl.ds(0, 8), :], edge_row.at[step, 1]
        else:
            src, dst = disp.at[step], edge_col.at[step, side - 2]
        return pltpu.make_async_remote_copy(
            src_ref=src,
            dst_ref=dst,
            send_sem=disp_send.at[step, side],
            recv_sem=disp_recv.at[step, side],
            device_id=at((-i, -j)),
            device_id_type=MESH,
        )

    pl.semaphore_wait(barrier, len(AROUND))
    for offset in AROUND:
        image_copy(offset).start()
    for side in range(4):
        disp_copy(0, side).start()

    sub64 = lax.broadcasted_iota(jnp.int32, (64, 128), 0)
    lane64 = lanes((64, 128))
    w2 = w2_ref[...].reshape(64, 9)
    for tap_col in range(3):
        spread = jnp.zeros((64, 128), F32)
        for tap_row in range(3):
            column = w2[:, 3 * tap_row + tap_col : 3 * tap_row + tap_col + 1]
            spread = jnp.where(
                lane64 == tap_row * 8 + (sub64 & 7), jnp.broadcast_to(column, (64, 128)), spread
            )
        base = jnp.sum(spread.reshape(8, 8, 128), axis=1)
        block = jnp.concatenate(
            [base if i == 0 else pltpu.roll(base, 8 * i, 1) for i in range(SLAB)], axis=0
        )
        high, low = split(block)
        at_row = tap_col * SLAB * 8
        toeplitz[at_row : at_row + SLAB * 8, 0:128] = high
        toeplitz[at_row : at_row + SLAB * 8, 128:256] = low
    w1 = w1_ref[...]
    taps = [jnp.broadcast_to(w1[:, k : k + 1], (8, 256)) for k in range(9)]
    sub8 = lax.broadcasted_iota(jnp.int32, (8, 256), 0)
    bias = jnp.zeros((8, 256), F32)
    for ch in range(CH):
        bias = jnp.where(sub8 == ch, b1_ref[ch], bias)

    for offset in AROUND:
        image_copy(offset).wait()

    full_rows, full_cols = rows_of_mesh * tile_rows, cols_of_mesh * tile_cols
    lane_tile = lanes((80, 128))

    def encode(which, first_lane, first_row, margin, slabs, store):
        def tile(slot):
            if slot == 4:
                return own[which].astype(F32)
            row, col = me_row + (slot // 3 - 1), me_col + (slot % 3 - 1)
            inside = (row >= 0) & (row < rows_of_mesh) & (col >= 0) & (col < cols_of_mesh)
            return around[slot, which].astype(F32) * jnp.where(inside, 1.0, 0.0).astype(F32)

        bands = []
        for col in range(3):
            bands.append(
                jnp.concatenate(
                    [tile(col)[8:, :], tile(3 + col), tile(6 + col)[: tile_rows - 8, :]], axis=0
                )
            )
        for tap_col in range(3):
            start = first_lane + tap_col
            if start == 128:
                left, right = bands[1], bands[2]
            else:
                turned = [pltpu.roll(x, 128 - start, 1) for x in bands]
                inside = lane_tile < 128 - start
                left = jnp.where(inside, turned[0], turned[1])
                right = jnp.where(inside, turned[1], turned[2])
            shifted[tap_col, :, 0:128] = left
            shifted[tap_col, :, 128:256] = right

        lane8 = lanes((8, 256))
        col8 = me_col * tile_cols + lane8 - (margin + 1)
        col_in = (col8 >= 0) & (col8 < full_cols)
        lane_e = lanes((SLAB * 8, 256))
        row_e = lax.broadcasted_iota(jnp.int32, (SLAB * 8, 256), 0) // 8
        col_e = me_col * tile_cols + lane_e - margin
        ok_col = (col_e >= 0) & (col_e < full_cols) & (lane_e < tile_cols + 2 * margin)

        for slab in slabs:
            hidden = []
            for i in range(SLAB + 2):
                h = bias
                for tap in range(9):
                    pixel = shifted[tap % 3, pl.ds(first_row + slab + i + tap // 3, 1), :]
                    h = h + taps[tap] * jnp.broadcast_to(pixel, (8, 256))
                row = me_row * tile_rows + (slab + i - margin - 1)
                row_ok = (row >= 0) & (row < full_rows)
                row_factor = jnp.where(row_ok, 1.0, 0.0).astype(F32)
                hidden.append(jnp.where(col_in, jnp.maximum(h, 0.0) * row_factor, 0.0))
            high, low = split(jnp.concatenate(hidden, axis=0))
            t_high, t_low = toeplitz[:, 0:128], toeplitz[:, 128:256]
            product = dot(
                jnp.concatenate([t_high, t_high], axis=1), jnp.concatenate([high, low], axis=0)
            ) + dot(t_low, high)
            n = SLAB * 8
            embed = (
                product[0:n]
                + pltpu.roll(product[n : 2 * n], 255, 1)
                + pltpu.roll(product[2 * n : 3 * n], 254, 1)
            )
            row_abs = me_row * tile_rows + row_e + (slab - margin)
            embed = jnp.where(ok_col & (row_abs >= 0) & (row_abs < full_rows), embed, 0.0)
            store(slab, embed)

    def halves(even, odd, low_half):
        axis = even.ndim - 1
        return (
            jnp.where(low_half, even, pltpu.roll(odd, 64, axis)),
            jnp.where(low_half, pltpu.roll(even, 64, axis), odd),
        )

    low8 = lanes((8, 128)) < 64

    def store_fixed(slab, embed):
        for pair in range(SLAB // 2):
            even = embed[pair * 16 : pair * 16 + 8, 0:128]
            odd = embed[pair * 16 + 8 : pair * 16 + 16, 0:128]
            left, right = halves(even, odd, low8)
            fixed_embed[slab // 2 + pair] = left
            fixed_embed[16 + slab // 2 + pair] = right

    low_e = lanes((SLAB * 8, 128)) < 64

    def store_moving(slab, embed):
        a, b = embed[:, 0:128], embed[:, 128:256]
        middle = jnp.where(low_e, pltpu.roll(a, 64, 1), pltpu.roll(b, 64, 1))
        for half, part in enumerate((a, middle)):
            high, low = split(part)
            lhs[half, slab * 8 : (slab + SLAB) * 8, 0:128] = high
            lhs[half, slab * 8 : (slab + SLAB) * 8, 128:256] = low

    encode(0, 126, 22, 0, (0, 14, 18), store_fixed)
    encode(1, 109, 5, REACH + 1, (0, 14, 28, 42, 52), store_moving)

    low16 = lanes((16, 128)) < 64
    lane32 = lanes((32, 128))
    position = (lane32 & 63).astype(F32) + (REACH + 1)
    second_row = jnp.where(lane32 >= 64, 1.0, 0.0).astype(F32)
    row32 = lax.broadcasted_iota(jnp.int32, (tile_rows, tile_cols), 0)
    has_north = jnp.where(me_row > 0, 1.0, 0.0).astype(F32)
    has_south = jnp.where(me_row < rows_of_mesh - 1, 1.0, 0.0).astype(F32)
    has_west = jnp.where(me_col > 0, 1.0, 0.0).astype(F32)
    has_east = jnp.where(me_col < cols_of_mesh - 1, 1.0, 0.0).astype(F32)

    def step(it, carry):
        grouped = []
        for comp in range(2):
            even = disp[it, comp, pl.ds(0, 16, stride=2), :]
            odd = disp[it, comp, pl.ds(1, 16, stride=2), :]
            grouped.append(jnp.concatenate(halves(even, odd, low16), axis=0))
        for comp in range(2):
            nearest = jnp.floor(grouped[comp] + 0.5)
            f = grouped[comp] - nearest
            at_w = 6 * comp
            weights[at_w] = 0.5 * (0.5 - f) * (0.5 - f)
            weights[at_w + 1] = 0.75 - f * f
            weights[at_w + 2] = 0.5 * (0.5 + f) * (0.5 + f)
            weights[at_w + 3] = f - 0.5
            weights[at_w + 4] = -2.0 * f
            weights[at_w + 5] = 0.5 + f
            if comp == 0:
                weights[12] = nearest + REACH + second_row
            else:
                weights[13] = nearest + position

        place = lax.broadcasted_iota(jnp.int32, (128, 128), 0).astype(F32)

        def sample(index, carry):
            half = index // 8
            quad = lax.rem(index, 8)
            columns = []
            for j in range(2):
                group = half * 16 + quad * 2 + j
                target = jnp.broadcast_to(weights[13, pl.ds(group, 1), :], (128, 128))
                off = place - target
                for b in range(3):
                    columns.append(jnp.where(off == b - 1, 1.0, 0.0).astype(BF16))
            onehot = jnp.concatenate(columns, axis=1)
            window = lhs[half, pl.ds(pl.multiple_of(quad * 32, 32), 304), :]
            picked = dot(window, jnp.concatenate([onehot, onehot], axis=0))
            for j in range(2):
                group = half * 16 + quad * 2 + j

                def weight(k):
                    return jnp.broadcast_to(weights[k, pl.ds(group, 1), :], (8, 128))

                offset = weight(12)
                masks = []
                for shift in (17, 8, 4, 2, 1, 1):
                    mask = offset >= shift
                    masks.append(mask)
                    offset = jnp.where(mask, offset - shift, offset)
                taps_at = []
                for b in range(3):
                    n = 3 * j + b
                    rows = [
                        picked[(2 * j + k) * 8 : (2 * j + k) * 8 + 8, n * 128 : n * 128 + 128]
                        for k in range(36)
                    ]
                    for shift, mask, count in zip(
                        (17, 8, 4, 2, 1, 1), masks, (19, 11, 7, 5, 4, 3)
                    ):
                        rows = [jnp.where(mask, rows[k + shift], rows[k]) for k in range(count)]
                    taps_at.append(rows)
                warped = slope_row = slope_col = None
                for b in range(3):
                    along = sum(weight(a) * taps_at[b][a] for a in range(3))
                    slant = sum(weight(3 + a) * taps_at[b][a] for a in range(3))
                    w, dw = weight(6 + b), weight(9 + b)
                    terms = (w * along, w * slant, dw * along)
                    if b == 0:
                        warped, slope_row, slope_col = terms
                    else:
                        warped += terms[0]
                        slope_row += terms[1]
                        slope_col += terms[2]
                mismatch = warped - fixed_embed[group]
                data[0, pl.ds(group, 1), :] = jnp.sum(mismatch * slope_row, axis=0, keepdims=True)
                data[1, pl.ds(group, 1), :] = jnp.sum(mismatch * slope_col, axis=0, keepdims=True)
            return carry

        lax.fori_loop(0, 16, sample, 0, unroll=8)

        for side in range(4):
            disp_copy(it, side).wait_recv()
        lane = lanes((tile_rows, tile_cols))
        one = jnp.where(it == 0, 1 / (1 - 0.9), jnp.where(it == 1, 1 / (1 - 0.9**2), 1 / (1 - 0.9**3)))
        two = jnp.where(
            it == 0, 1 / (1 - 0.999), jnp.where(it == 1, 1 / (1 - 0.999**2), 1 / (1 - 0.999**3))
        )
        for comp in range(2):
            even, odd = halves(data[comp, 0:16, :], data[comp, 16:32, :], low16)
            out_ref[comp, pl.ds(0, 16, stride=2), :] = even
            out_ref[comp, pl.ds(1, 16, stride=2), :] = odd
            sampled = out_ref[comp] * (2.0 / CH)
            d = disp[it, comp]
            north = jnp.where(
                row32 == 0, has_north * edge_row[it, 0, comp, 7:8, :], pltpu.roll(d, 1, 0)
            )
            south = jnp.where(
                row32 == tile_rows - 1,
                has_south * edge_row[it, 1, comp, 0:1, :],
                pltpu.roll(d, tile_rows - 1, 0),
            )
            west = pltpu.roll(
                jnp.where(lane == tile_cols - 1, has_west * edge_col[it, 0, comp], d), 1, 1
            )
            east = pltpu.roll(
                jnp.where(lane == 0, has_east * edge_col[it, 1, comp], d), tile_cols - 1, 1
            )
            squashed = d * (1.0 / REACH)
            gradient = (
                sampled + 2.0 * stiffness * (4.0 * d - (south + north + east + west))
            ) * (1.0 - squashed * squashed)
            m1 = 0.9 * first_moment[comp] + 0.1 * gradient
            m2 = 0.999 * second_moment[comp] + 0.001 * gradient * gradient
            first_moment[comp] = m1
            second_moment[comp] = m2
            new = raw[comp] - step_size * (m1 * one) / (jnp.sqrt(m2 * two) + adam_epsilon)
            raw[comp] = new

            @pl.when(it < ITERS - 1)
            def _():
                disp[it + 1, comp] = REACH * jnp.tanh(new / REACH)

        @pl.when(it < ITERS - 1)
        def _():
            for side in range(4):
                disp_copy(it + 1, side).start()

        return carry

    lax.fori_loop(0, ITERS, step, 0)
    out_ref[...] = raw[...] - field_ref[...]
    for it in range(ITERS):
        for side in range(4):
            disp_copy(it, side).wait_send()


def local(rows_of_mesh, cols_of_mesh, fixed, moving, field, w1, b1, w2):
    tile_rows, tile_cols = fixed.shape
    vmem = pl.BlockSpec(memory_space=pltpu.VMEM)
    tile = (tile_rows, tile_cols)
    return pl.pallas_call(
        functools.partial(kernel, rows_of_mesh, cols_of_mesh),
        out_shape=jax.ShapeDtypeStruct(field.shape, F32),
        in_specs=[pl.BlockSpec(memory_space=pltpu.HBM)] * 6,
        out_specs=vmem,
        scratch_shapes=[
            pltpu.VMEM(field.shape, F32),
            pltpu.VMEM(w1.shape, F32),
            pltpu.SMEM(b1.shape, F32),
            pltpu.VMEM(w2.shape, F32),
            pltpu.VMEM((2,) + tile, BF16),
            pltpu.VMEM((9, 2) + tile, BF16),
            pltpu.VMEM((3, 80, 256), F32),
            pltpu.VMEM((3 * SLAB * 8, 256), BF16),
            pltpu.VMEM((2, 66 * 8, 256), BF16),
            pltpu.VMEM((32, 8, 128), F32),
            pltpu.VMEM((ITERS, 2) + tile, F32),
            pltpu.VMEM((ITERS, 2, 2, 8, tile_cols), F32),
            pltpu.VMEM((ITERS, 2, 2) + tile, F32),
            pltpu.VMEM((2,) + tile, F32),
            pltpu.VMEM((2,) + tile, F32),
            pltpu.VMEM((2,) + tile, F32),
            pltpu.VMEM((14, 32, 128), F32),
            pltpu.VMEM((2, 32, 128), F32),
            pltpu.SemaphoreType.DMA((9,)),
            pltpu.SemaphoreType.DMA((9,)),
            pltpu.SemaphoreType.DMA((ITERS, 4)),
            pltpu.SemaphoreType.DMA((ITERS, 4)),
            pltpu.SemaphoreType.DMA((6,)),
        ],
        compiler_params=pltpu.CompilerParams(
            collective_id=0, has_side_effects=True, vmem_limit_bytes=60 << 20
        ),
        name="refine",
    )(fixed, moving, field, w1, b1, w2)


def solution(mesh):
    return jax.shard_map(
        functools.partial(local, mesh.shape["row"], mesh.shape["col"]),
        mesh=mesh,
        in_specs=(P("row", "col"), P("row", "col"), P(None, "row", "col"), P(), P(), P()),
        out_specs=P(None, "row", "col"),
        check_vma=False,
    )
```

```python
import functools

import jax
import jax.numpy as jnp
from jax import lax
from jax.experimental import pallas as pl
from jax.experimental.pallas import tpu as pltpu
from jax.sharding import PartitionSpec as P

REACH = 16
ITERS = 3
CH = 8

stiffness = 0.01
step_size = 0.5
adam_epsilon = 0.01

F32 = jnp.float32
BF16 = jnp.bfloat16
MESH = pl.DeviceIdType.MESH
AROUND = [(i, j) for i in (-1, 0, 1) for j in (-1, 0, 1) if (i, j) != (0, 0)]
SIDES = [(-1, 0), (1, 0), (0, -1), (0, 1)]
SLAB = 14


def lanes(shape):
    return lax.broadcasted_iota(jnp.int32, shape, len(shape) - 1)


def split(x):
    high = x.astype(BF16)
    return high, (x - high.astype(F32)).astype(BF16)


def dot(a, b):
    return lax.dot_general(a, b, (((1,), (0,)), ((), ())), preferred_element_type=F32)


def kernel(
    rows_of_mesh,
    cols_of_mesh,
    fixed_hbm,
    moving_hbm,
    field_hbm,
    w1_hbm,
    b1_hbm,
    w2_hbm,
    out_ref,
    field_ref,
    w1_ref,
    b1_ref,
    w2_ref,
    own,
    around,
    shifted,
    toeplitz,
    lhs,
    fixed_embed,
    disp,
    edge_row,
    edge_col,
    raw,
    first_moment,
    second_moment,
    weights,
    data,
    image_send,
    image_recv,
    disp_send,
    disp_recv,
    load_sem,
):
    me_row, me_col = lax.axis_index("row"), lax.axis_index("col")
    tile_rows, tile_cols = fixed_hbm.shape

    def at(offset):
        return me_row + offset[0], me_col + offset[1]

    def present(offset):
        row, col = at(offset)
        return (row >= 0) & (row < rows_of_mesh) & (col >= 0) & (col < cols_of_mesh)

    barrier = pltpu.get_barrier_semaphore()
    for offset in AROUND:

        @pl.when(present(offset))
        def _():
            pl.semaphore_signal(barrier, inc=1, device_id=at(offset), device_id_type=MESH)

    loads = [
        pltpu.make_async_copy(src, dst, load_sem.at[i])
        for i, (src, dst) in enumerate(
            [
                (field_hbm, field_ref),
                (moving_hbm, own.at[1]),
                (fixed_hbm, own.at[0]),
                (w2_hbm, w2_ref),
                (w1_hbm, w1_ref),
                (b1_hbm, b1_ref),
            ]
        )
    ]
    for load in loads:
        load.start()
    for offset in AROUND:
        slot = 3 * (offset[0] + 1) + offset[1] + 1

        @pl.when(jnp.logical_not(present(offset)))
        def _():
            around[slot] = jnp.zeros(around.shape[1:], BF16)

    for side in range(4):

        @pl.when(jnp.logical_not(present(SIDES[side])))
        def _():
            if side < 2:
                edge_row[:, side] = jnp.zeros((ITERS,) + edge_row.shape[2:], F32)
            else:
                edge_col[:, side - 2] = jnp.zeros((ITERS,) + edge_col.shape[2:], F32)

    first_moment[...] = jnp.zeros_like(first_moment)
    second_moment[...] = jnp.zeros_like(second_moment)
    loads[0].wait()
    raw[...] = field_ref[...]
    disp[0] = REACH * jnp.tanh(field_ref[...] / REACH)
    for load in loads[1:]:
        load.wait()

    def image_copy(slot):
        i, j = 1 - slot // 3, 1 - slot % 3
        return pltpu.make_async_remote_copy(
            src_ref=own,
            dst_ref=around.at[slot],
            send_sem=image_send.at[slot],
            recv_sem=image_recv.at[slot],
            device_id=at((i, j)),
            device_id_type=MESH,
        )

    def disp_copy(step, side):
        i, j = SIDES[side]
        if side == 0:
            src, dst = disp.at[step, :, pl.ds(tile_rows - 8, 8), :], edge_row.at[step, 0]
        elif side == 1:
            src, dst = disp.at[step, :, pl.ds(0, 8), :], edge_row.at[step, 1]
        else:
            src, dst = disp.at[step], edge_col.at[step, side - 2]
        return pltpu.make_async_remote_copy(
            src_ref=src,
            dst_ref=dst,
            send_sem=disp_send.at[step, side],
            recv_sem=disp_recv.at[step, side],
            device_id=at((-i, -j)),
            device_id_type=MESH,
        )

    def send_disp(step):
        for side in range(4):
            i, j = SIDES[side]

            @pl.when(present((-i, -j)))
            def _():
                disp_copy(step, side).start()

    rows_near = 1 + (me_row > 0).astype(jnp.int32) + (me_row < rows_of_mesh - 1).astype(jnp.int32)
    cols_near = 1 + (me_col > 0).astype(jnp.int32) + (me_col < cols_of_mesh - 1).astype(jnp.int32)
    pl.semaphore_wait(barrier, rows_near * cols_near - 1)
    for i, j in AROUND:

        @pl.when(present((-i, -j)))
        def _():
            image_copy(3 * (i + 1) + j + 1).start()

    send_disp(0)

    sub64 = lax.broadcasted_iota(jnp.int32, (64, 128), 0)
    lane64 = lanes((64, 128))
    w2 = w2_ref[...].reshape(64, 9)
    for tap_col in range(3):
        spread = jnp.zeros((64, 128), F32)
        for tap_row in range(3):
            column = w2[:, 3 * tap_row + tap_col : 3 * tap_row + tap_col + 1]
            spread = jnp.where(
                lane64 == tap_row * 8 + (sub64 & 7), jnp.broadcast_to(column, (64, 128)), spread
            )
        base = jnp.sum(spread.reshape(8, 8, 128), axis=1)
        block = jnp.concatenate(
            [base if i == 0 else pltpu.roll(base, 8 * i, 1) for i in range(SLAB)], axis=0
        )
        high, low = split(block)
        at_row = tap_col * SLAB * 8
        toeplitz[at_row : at_row + SLAB * 8, 0:128] = high
        toeplitz[at_row : at_row + SLAB * 8, 128:256] = low
    w1 = w1_ref[...]
    taps = [jnp.broadcast_to(w1[:, k : k + 1], (8, 256)) for k in range(9)]
    sub8 = lax.broadcasted_iota(jnp.int32, (8, 256), 0)
    bias = jnp.zeros((8, 256), F32)
    for ch in range(CH):
        bias = jnp.where(sub8 == ch, b1_ref[ch], bias)

    for i, j in AROUND:

        @pl.when(present((i, j)))
        def _():
            image_copy(3 * (i + 1) + j + 1).wait_recv()

    full_rows, full_cols = rows_of_mesh * tile_rows, cols_of_mesh * tile_cols
    lane_tile = lanes((80, 128))

    def encode(which, first_lane, first_row, margin, slabs, store):
        def tile(slot):
            if slot == 4:
                return own[which].astype(F32)
            return around[slot, which].astype(F32)

        bands = []
        for col in range(3):
            bands.append(
                jnp.concatenate(
                    [tile(col)[8:, :], tile(3 + col), tile(6 + col)[: tile_rows - 8, :]], axis=0
                )
            )
        for tap_col in range(3):
            start = first_lane + tap_col
            if start == 128:
                left, right = bands[1], bands[2]
            else:
                turned = [pltpu.roll(x, 128 - start, 1) for x in bands]
                inside = lane_tile < 128 - start
                left = jnp.where(inside, turned[0], turned[1])
                right = jnp.where(inside, turned[1], turned[2])
            shifted[tap_col, :, 0:128] = left
            shifted[tap_col, :, 128:256] = right

        lane8 = lanes((8, 256))
        col8 = me_col * tile_cols + lane8 - (margin + 1)
        col_in = (col8 >= 0) & (col8 < full_cols)
        lane_e = lanes((SLAB * 8, 256))
        row_e = lax.broadcasted_iota(jnp.int32, (SLAB * 8, 256), 0) // 8
        col_e = me_col * tile_cols + lane_e - margin
        ok_col = (col_e >= 0) & (col_e < full_cols) & (lane_e < tile_cols + 2 * margin)

        for slab in slabs:
            hidden = []
            for i in range(SLAB + 2):
                h = bias
                for tap in range(9):
                    pixel = shifted[tap % 3, pl.ds(first_row + slab + i + tap // 3, 1), :]
                    h = h + taps[tap] * jnp.broadcast_to(pixel, (8, 256))
                row = me_row * tile_rows + (slab + i - margin - 1)
                row_ok = (row >= 0) & (row < full_rows)
                row_factor = jnp.where(row_ok, 1.0, 0.0).astype(F32)
                hidden.append(jnp.where(col_in, jnp.maximum(h, 0.0) * row_factor, 0.0))
            high, low = split(jnp.concatenate(hidden, axis=0))
            t_high, t_low = toeplitz[:, 0:128], toeplitz[:, 128:256]
            product = dot(
                jnp.concatenate([t_high, t_high], axis=1), jnp.concatenate([high, low], axis=0)
            ) + dot(t_low, high)
            n = SLAB * 8
            embed = (
                product[0:n]
                + pltpu.roll(product[n : 2 * n], 255, 1)
                + pltpu.roll(product[2 * n : 3 * n], 254, 1)
            )
            row_abs = me_row * tile_rows + row_e + (slab - margin)
            embed = jnp.where(ok_col & (row_abs >= 0) & (row_abs < full_rows), embed, 0.0)
            store(slab, embed)

    def halves(even, odd, low_half):
        axis = even.ndim - 1
        return (
            jnp.where(low_half, even, pltpu.roll(odd, 64, axis)),
            jnp.where(low_half, pltpu.roll(even, 64, axis), odd),
        )

    low8 = lanes((8, 128)) < 64

    def store_fixed(slab, embed):
        for pair in range(SLAB // 2):
            even = embed[pair * 16 : pair * 16 + 8, 0:128]
            odd = embed[pair * 16 + 8 : pair * 16 + 16, 0:128]
            left, right = halves(even, odd, low8)
            fixed_embed[slab // 2 + pair] = left
            fixed_embed[16 + slab // 2 + pair] = right

    low_e = lanes((SLAB * 8, 128)) < 64

    def store_moving(slab, embed):
        a, b = embed[:, 0:128], embed[:, 128:256]
        middle = jnp.where(low_e, pltpu.roll(a, 64, 1), pltpu.roll(b, 64, 1))
        for half, part in enumerate((a, middle)):
            high, low = split(part)
            lhs[half, slab * 8 : (slab + SLAB) * 8, 0:128] = high
            lhs[half, slab * 8 : (slab + SLAB) * 8, 128:256] = low

    encode(0, 126, 22, 0, (0, 14, 18), store_fixed)
    encode(1, 109, 5, REACH + 1, (0, 14, 28, 42, 52), store_moving)

    low16 = lanes((16, 128)) < 64
    lane32 = lanes((32, 128))
    position = (lane32 & 63).astype(F32) + (REACH + 1)
    second_row = jnp.where(lane32 >= 64, 1.0, 0.0).astype(F32)
    row32 = lax.broadcasted_iota(jnp.int32, (tile_rows, tile_cols), 0)

    def step(it, carry):
        grouped = []
        for comp in range(2):
            even = disp[it, comp, pl.ds(0, 16, stride=2), :]
            odd = disp[it, comp, pl.ds(1, 16, stride=2), :]
            grouped.append(jnp.concatenate(halves(even, odd, low16), axis=0))
        for comp in range(2):
            nearest = jnp.floor(grouped[comp] + 0.5)
            f = grouped[comp] - nearest
            at_w = 6 * comp
            weights[at_w] = 0.5 * (0.5 - f) * (0.5 - f)
            weights[at_w + 1] = 0.75 - f * f
            weights[at_w + 2] = 0.5 * (0.5 + f) * (0.5 + f)
            weights[at_w + 3] = f - 0.5
            weights[at_w + 4] = -2.0 * f
            weights[at_w + 5] = 0.5 + f
            if comp == 0:
                weights[12] = nearest + REACH + second_row
            else:
                weights[13] = nearest + position

        place = lax.broadcasted_iota(jnp.int32, (128, 128), 0).astype(F32)

        def sample(index, carry):
            half = index // 8
            quad = lax.rem(index, 8)
            columns = []
            for j in range(2):
                group = half * 16 + quad * 2 + j
                target = jnp.broadcast_to(weights[13, pl.ds(group, 1), :], (128, 128))
                off = place - target
                for b in range(3):
                    columns.append(jnp.where(off == b - 1, 1.0, 0.0).astype(BF16))
            onehot = jnp.concatenate(columns, axis=1)
            window = lhs[half, pl.ds(pl.multiple_of(quad * 32, 32), 304), :]
            picked = dot(window, jnp.concatenate([onehot, onehot], axis=0))
            for j in range(2):
                group = half * 16 + quad * 2 + j

                def weight(k):
                    return jnp.broadcast_to(weights[k, pl.ds(group, 1), :], (8, 128))

                offset = weight(12)
                masks = []
                for shift in (17, 8, 4, 2, 1, 1):
                    mask = offset >= shift
                    masks.append(mask)
                    offset = jnp.where(mask, offset - shift, offset)
                taps_at = []
                for b in range(3):
                    n = 3 * j + b
                    rows = [
                        picked[(2 * j + k) * 8 : (2 * j + k) * 8 + 8, n * 128 : n * 128 + 128]
                        for k in range(36)
                    ]
                    for shift, mask, count in zip(
                        (17, 8, 4, 2, 1, 1), masks, (19, 11, 7, 5, 4, 3)
                    ):
                        rows = [jnp.where(mask, rows[k + shift], rows[k]) for k in range(count)]
                    taps_at.append(rows)
                warped = slope_row = slope_col = None
                for b in range(3):
                    along = sum(weight(a) * taps_at[b][a] for a in range(3))
                    slant = sum(weight(3 + a) * taps_at[b][a] for a in range(3))
                    w, dw = weight(6 + b), weight(9 + b)
                    terms = (w * along, w * slant, dw * along)
                    if b == 0:
                        warped, slope_row, slope_col = terms
                    else:
                        warped += terms[0]
                        slope_row += terms[1]
                        slope_col += terms[2]
                mismatch = warped - fixed_embed[group]
                data[0, pl.ds(group, 1), :] = jnp.sum(mismatch * slope_row, axis=0, keepdims=True)
                data[1, pl.ds(group, 1), :] = jnp.sum(mismatch * slope_col, axis=0, keepdims=True)
            return carry

        lax.fori_loop(0, 16, sample, 0, unroll=8)

        for side in range(4):

            @pl.when(present(SIDES[side]))
            def _():
                disp_copy(it, side).wait_recv()

        lane = lanes((tile_rows, tile_cols))
        one = jnp.where(it == 0, 1 / (1 - 0.9), jnp.where(it == 1, 1 / (1 - 0.9**2), 1 / (1 - 0.9**3)))
        two = jnp.where(
            it == 0, 1 / (1 - 0.999), jnp.where(it == 1, 1 / (1 - 0.999**2), 1 / (1 - 0.999**3))
        )
        for comp in range(2):
            even, odd = halves(data[comp, 0:16, :], data[comp, 16:32, :], low16)
            out_ref[comp, pl.ds(0, 16, stride=2), :] = even
            out_ref[comp, pl.ds(1, 16, stride=2), :] = odd
            sampled = out_ref[comp] * (2.0 / CH)
            d = disp[it, comp]
            north = jnp.where(
                row32 == 0, edge_row[it, 0, comp, 7:8, :], pltpu.roll(d, 1, 0)
            )
            south = jnp.where(
                row32 == tile_rows - 1,
                edge_row[it, 1, comp, 0:1, :],
                pltpu.roll(d, tile_rows - 1, 0),
            )
            west = pltpu.roll(
                jnp.where(lane == tile_cols - 1, edge_col[it, 0, comp], d), 1, 1
            )
            east = pltpu.roll(
                jnp.where(lane == 0, edge_col[it, 1, comp], d), tile_cols - 1, 1
            )
            squashed = d * (1.0 / REACH)
            gradient = (
                sampled + 2.0 * stiffness * (4.0 * d - (south + north + east + west))
            ) * (1.0 - squashed * squashed)
            m1 = 0.9 * first_moment[comp] + 0.1 * gradient
            m2 = 0.999 * second_moment[comp] + 0.001 * gradient * gradient
            first_moment[comp] = m1
            second_moment[comp] = m2
            new = raw[comp] - step_size * (m1 * one) / (jnp.sqrt(m2 * two) + adam_epsilon)
            raw[comp] = new

            @pl.when(it < ITERS - 1)
            def _():
                disp[it + 1, comp] = REACH * jnp.tanh(new / REACH)

        @pl.when(it < ITERS - 1)
        def _():
            send_disp(it + 1)

        return carry

    lax.fori_loop(0, ITERS, step, 0)
    out_ref[...] = raw[...] - field_ref[...]
    for i, j in AROUND:

        @pl.when(present((-i, -j)))
        def _():
            image_copy(3 * (i + 1) + j + 1).wait_send()

    for side in range(4):
        i, j = SIDES[side]

        @pl.when(present((-i, -j)))
        def _():
            for it in range(ITERS):
                disp_copy(it, side).wait_send()


def local(rows_of_mesh, cols_of_mesh, fixed, moving, field, w1, b1, w2):
    tile_rows, tile_cols = fixed.shape
    vmem = pl.BlockSpec(memory_space=pltpu.VMEM)
    tile = (tile_rows, tile_cols)
    return pl.pallas_call(
        functools.partial(kernel, rows_of_mesh, cols_of_mesh),
        out_shape=jax.ShapeDtypeStruct(field.shape, F32),
        in_specs=[pl.BlockSpec(memory_space=pltpu.HBM)] * 6,
        out_specs=vmem,
        scratch_shapes=[
            pltpu.VMEM(field.shape, F32),
            pltpu.VMEM(w1.shape, F32),
            pltpu.SMEM(b1.shape, F32),
            pltpu.VMEM(w2.shape, F32),
            pltpu.VMEM((2,) + tile, BF16),
            pltpu.VMEM((9, 2) + tile, BF16),
            pltpu.VMEM((3, 80, 256), F32),
            pltpu.VMEM((3 * SLAB * 8, 256), BF16),
            pltpu.VMEM((2, 66 * 8, 256), BF16),
            pltpu.VMEM((32, 8, 128), F32),
            pltpu.VMEM((ITERS, 2) + tile, F32),
            pltpu.VMEM((ITERS, 2, 2, 8, tile_cols), F32),
            pltpu.VMEM((ITERS, 2, 2) + tile, F32),
            pltpu.VMEM((2,) + tile, F32),
            pltpu.VMEM((2,) + tile, F32),
            pltpu.VMEM((2,) + tile, F32),
            pltpu.VMEM((14, 32, 128), F32),
            pltpu.VMEM((2, 32, 128), F32),
            pltpu.SemaphoreType.DMA((9,)),
            pltpu.SemaphoreType.DMA((9,)),
            pltpu.SemaphoreType.DMA((ITERS, 4)),
            pltpu.SemaphoreType.DMA((ITERS, 4)),
            pltpu.SemaphoreType.DMA((6,)),
        ],
        compiler_params=pltpu.CompilerParams(
            collective_id=0, has_side_effects=True, vmem_limit_bytes=60 << 20
        ),
        name="refine",
    )(fixed, moving, field, w1, b1, w2)


def solution(mesh):
    return jax.shard_map(
        functools.partial(local, mesh.shape["row"], mesh.shape["col"]),
        mesh=mesh,
        in_specs=(P("row", "col"), P("row", "col"), P(None, "row", "col"), P(), P(), P()),
        out_specs=P(None, "row", "col"),
        check_vma=False,
    )
```

```python
import functools

import jax
import jax.numpy as jnp
from jax import lax
from jax.experimental import pallas as pl
from jax.experimental.pallas import tpu as pltpu
from jax.sharding import PartitionSpec as P

REACH = 16
ITERS = 3
CH = 8

stiffness = 0.01
step_size = 0.5
adam_epsilon = 0.01

F32 = jnp.float32
BF16 = jnp.bfloat16
MESH = pl.DeviceIdType.MESH
AROUND = [(i, j) for i in (-1, 0, 1) for j in (-1, 0, 1) if (i, j) != (0, 0)]
NORTH_SOUTH = [(-1, 0), (1, 0)]
WEST_EAST = [(0, -1), (0, 1)]
HALO = 8
EXTRA = 2
SLAB = 14


def lanes(shape):
    return lax.broadcasted_iota(jnp.int32, shape, len(shape) - 1)


def split(x):
    high = x.astype(BF16)
    return high, (x - high.astype(F32)).astype(BF16)


def dot(a, b):
    return lax.dot_general(a, b, (((1,), (0,)), ((), ())), preferred_element_type=F32)


def kernel(
    rows_of_mesh,
    cols_of_mesh,
    fixed_hbm,
    moving_hbm,
    field_hbm,
    w1_hbm,
    b1_hbm,
    w2_hbm,
    out_ref,
    field_ref,
    w1_ref,
    b1_ref,
    w2_ref,
    own,
    around,
    shifted,
    toeplitz,
    lhs,
    lhs_f32,
    fixed_embed,
    disp,
    edge_col,
    raw,
    first_moment,
    second_moment,
    weights,
    data,
    unpaired,
    image_send,
    image_recv,
    field_send,
    field_recv,
    disp_send,
    disp_recv,
    load_sem,
):
    me_row, me_col = lax.axis_index("row"), lax.axis_index("col")
    tile_rows, tile_cols = fixed_hbm.shape
    ext_rows = tile_rows + 2 * HALO

    def at(offset):
        return me_row + offset[0], me_col + offset[1]

    def present(offset):
        row, col = at(offset)
        return (row >= 0) & (row < rows_of_mesh) & (col >= 0) & (col < cols_of_mesh)

    barrier = pltpu.get_barrier_semaphore()
    for offset in AROUND:

        @pl.when(present(offset))
        def _():
            pl.semaphore_signal(barrier, inc=1, device_id=at(offset), device_id_type=MESH)

    loads = [
        pltpu.make_async_copy(src, dst, load_sem.at[i])
        for i, (src, dst) in enumerate(
            [
                (field_hbm, field_ref.at[:, pl.ds(HALO, tile_rows), :]),
                (moving_hbm, own.at[1]),
                (fixed_hbm, own.at[0]),
                (w2_hbm, w2_ref),
                (w1_hbm, w1_ref),
                (b1_hbm, b1_ref),
            ]
        )
    ]
    for load in loads:
        load.start()
    for offset in AROUND:
        slot = 3 * (offset[0] + 1) + offset[1] + 1

        @pl.when(jnp.logical_not(present(offset)))
        def _():
            around[slot] = jnp.zeros(around.shape[1:], BF16)

    for side in range(2):

        @pl.when(jnp.logical_not(present(NORTH_SOUTH[side])))
        def _():
            at_row = side * (HALO + tile_rows)
            field_ref[:, at_row : at_row + HALO, :] = jnp.zeros((2, HALO, tile_cols), F32)

        @pl.when(jnp.logical_not(present(WEST_EAST[side])))
        def _():
            edge_col[:, side] = jnp.zeros((ITERS,) + edge_col.shape[2:], F32)

    data[...] = jnp.zeros_like(data)
    first_moment[...] = jnp.zeros_like(first_moment)
    second_moment[...] = jnp.zeros_like(second_moment)

    def image_copies(slot):
        i, j = 1 - slot // 3, 1 - slot % 3
        return [
            pltpu.make_async_remote_copy(
                src_ref=own,
                dst_ref=around.at[slot],
                send_sem=image_send.at[0, slot],
                recv_sem=image_recv.at[0, slot],
                device_id=at((i, j)),
                device_id_type=MESH,
            )
        ]

    def field_copy(side):
        i, _ = NORTH_SOUTH[side]
        return pltpu.make_async_remote_copy(
            src_ref=field_hbm.at[:, pl.ds((tile_rows - HALO) * (1 - side), HALO), :],
            dst_ref=field_ref.at[:, pl.ds((HALO + tile_rows) * side, HALO), :],
            send_sem=field_send.at[side],
            recv_sem=field_recv.at[side],
            device_id=at((-i, 0)),
            device_id_type=MESH,
        )

    def disp_copy(step, side):
        _, j = WEST_EAST[side]
        return pltpu.make_async_remote_copy(
            src_ref=disp.at[step],
            dst_ref=edge_col.at[step, side],
            send_sem=disp_send.at[step, side],
            recv_sem=disp_recv.at[step, side],
            device_id=at((0, -j)),
            device_id_type=MESH,
        )

    def send_disp(step):
        for side in range(2):

            @pl.when(present(WEST_EAST[1 - side]))
            def _():
                disp_copy(step, side).start()

    for load in loads:
        load.wait()

    rows_near = 1 + (me_row > 0).astype(jnp.int32) + (me_row < rows_of_mesh - 1).astype(jnp.int32)
    cols_near = 1 + (me_col > 0).astype(jnp.int32) + (me_col < cols_of_mesh - 1).astype(jnp.int32)
    pl.semaphore_wait(barrier, rows_near * cols_near - 1)
    for i, j in AROUND:

        @pl.when(present((-i, -j)))
        def _():
            for copy in image_copies(3 * (i + 1) + j + 1):
                copy.start()

    for side in range(2):

        @pl.when(present(NORTH_SOUTH[1 - side]))
        def _():
            field_copy(side).start()

    sub64 = lax.broadcasted_iota(jnp.int32, (64, 128), 0)
    lane64 = lanes((64, 128))
    w2 = w2_ref[...].reshape(64, 9)
    for tap_col in range(3):
        spread = jnp.zeros((64, 128), F32)
        for tap_row in range(3):
            column = w2[:, 3 * tap_row + tap_col : 3 * tap_row + tap_col + 1]
            spread = jnp.where(
                lane64 == tap_row * 8 + (sub64 & 7), jnp.broadcast_to(column, (64, 128)), spread
            )
        base = jnp.sum(spread.reshape(8, 8, 128), axis=1)
        block = jnp.concatenate(
            [base if i == 0 else pltpu.roll(base, 8 * i, 1) for i in range(SLAB)], axis=0
        )
        high, low = split(block)
        at_row = tap_col * SLAB * 8
        toeplitz[at_row : at_row + SLAB * 8, 0:128] = high
        toeplitz[at_row : at_row + SLAB * 8, 128:256] = low
    w1 = w1_ref[...]
    taps = [jnp.broadcast_to(w1[:, k : k + 1], (8, 256)) for k in range(9)]
    sub8 = lax.broadcasted_iota(jnp.int32, (8, 256), 0)
    bias = jnp.zeros((8, 256), F32)
    for ch in range(CH):
        bias = jnp.where(sub8 == ch, b1_ref[ch], bias)

    for side in range(2):

        @pl.when(present(NORTH_SOUTH[side]))
        def _():
            field_copy(side).wait_recv()

    full_rows, full_cols = rows_of_mesh * tile_rows, cols_of_mesh * tile_cols
    row_ext = me_row * tile_rows - HALO + lax.broadcasted_iota(
        jnp.int32, (ext_rows, tile_cols), 0
    )
    in_section = (row_ext >= 0) & (row_ext < full_rows)
    for comp in range(2):
        raw[comp] = field_ref[comp]
        disp[0, comp] = jnp.where(in_section, REACH * jnp.tanh(field_ref[comp] / REACH), 0.0)
    send_disp(0)

    for i, j in AROUND:

        @pl.when(present((i, j)))
        def _():
            for copy in image_copies(3 * (i + 1) + j + 1):
                copy.wait_recv()

    lane_tile = lanes((80, 128))

    def encode(which, first_lane, first_row, row_margin, margin, slabs, store):
        def tile(slot):
            if slot == 4:
                return own[which].astype(F32)
            return around[slot, which].astype(F32)

        bands = []
        for col in range(3):
            bands.append(
                jnp.concatenate(
                    [tile(col)[8:, :], tile(3 + col), tile(6 + col)[: tile_rows - 8, :]], axis=0
                )
            )
        for tap_col in range(3):
            start = first_lane + tap_col
            if start == 128:
                left, right = bands[1], bands[2]
            else:
                turned = [pltpu.roll(x, 128 - start, 1) for x in bands]
                inside = lane_tile < 128 - start
                left = jnp.where(inside, turned[0], turned[1])
                right = jnp.where(inside, turned[1], turned[2])
            shifted[tap_col, :, 0:128] = left
            shifted[tap_col, :, 128:256] = right

        lane8 = lanes((8, 256))
        col8 = me_col * tile_cols + lane8 - (margin + 1)
        col_in = (col8 >= 0) & (col8 < full_cols)
        lane_e = lanes((SLAB * 8, 256))
        row_e = lax.broadcasted_iota(jnp.int32, (SLAB * 8, 256), 0) // 8
        col_e = me_col * tile_cols + lane_e - margin
        ok_col = (col_e >= 0) & (col_e < full_cols) & (lane_e < tile_cols + 2 * margin)

        for slab in slabs:
            hidden = []
            pixels = {}
            for i in range(SLAB + 4):
                for tap_col in range(3):
                    pixel = shifted[tap_col, pl.ds(first_row + slab + i, 1), :]
                    pixels[i, tap_col] = jnp.broadcast_to(pixel, (8, 256))
            for i in range(SLAB + 2):
                h = bias
                for tap in range(9):
                    h = h + taps[tap] * pixels[i + tap // 3, tap % 3]
                row = me_row * tile_rows + (slab + i - row_margin - 1)
                row_ok = (row >= 0) & (row < full_rows)
                row_factor = jnp.where(row_ok, 1.0, 0.0).astype(F32)
                hidden.append(jnp.where(col_in, jnp.maximum(h, 0.0) * row_factor, 0.0))
            high, low = split(jnp.concatenate(hidden, axis=0))
            t_high, t_low = toeplitz[:, 0:128], toeplitz[:, 128:256]
            product = dot(
                jnp.concatenate([t_high, t_high], axis=1), jnp.concatenate([high, low], axis=0)
            ) + dot(t_low, high)
            n = SLAB * 8
            embed = (
                product[0:n]
                + pltpu.roll(product[n : 2 * n], 255, 1)
                + pltpu.roll(product[2 * n : 3 * n], 254, 1)
            )
            row_abs = me_row * tile_rows + row_e + (slab - row_margin)
            embed = jnp.where(ok_col & (row_abs >= 0) & (row_abs < full_rows), embed, 0.0)
            store(slab, embed)

    def halves(even, odd, low_half):
        axis = even.ndim - 1
        return (
            jnp.where(low_half, even, pltpu.roll(odd, 64, axis)),
            jnp.where(low_half, pltpu.roll(even, 64, axis), odd),
        )

    low8 = lanes((8, 128)) < 64
    pairs = ext_rows // 2
    first_pair = (HALO - EXTRA) // 2

    def store_fixed(slab, embed):
        for pair in range(SLAB // 2):
            even = embed[pair * 16 : pair * 16 + 8, 0:128]
            odd = embed[pair * 16 + 8 : pair * 16 + 16, 0:128]
            left, right = halves(even, odd, low8)
            at_pair = first_pair + slab // 2 + pair
            fixed_embed[at_pair] = left
            fixed_embed[pairs + at_pair] = right

    low_e = lanes((SLAB * 8, 128)) < 64

    def store_moving(slab, embed):
        a, b = embed[:, 0:128], embed[:, 128:256]
        middle = jnp.where(low_e, pltpu.roll(a, 64, 1), pltpu.roll(b, 64, 1))
        for half, part in enumerate((a, middle)):
            lhs_f32[half, slab * 8 : (slab + SLAB) * 8, :] = part
            high, low = split(part)
            lhs[half, slab * 8 : (slab + SLAB) * 8, 0:128] = high
            lhs[half, slab * 8 : (slab + SLAB) * 8, 128:256] = low

    encode(0, 126, 24 - EXTRA - 2, EXTRA, 0, (0, 14, 22), store_fixed)
    encode(
        1, 109, 24 - EXTRA - REACH - 3, EXTRA + REACH + 1, REACH + 1, (0, 14, 28, 42, 56), store_moving
    )

    low_half = lanes((pairs, 128)) < 64
    lane_g = lanes((2 * pairs, 128))
    position = (lane_g & 63).astype(F32) + (REACH + 1)
    second_row = jnp.where(lane_g >= 64, 1.0, 0.0).astype(F32)

    def step(it, start, triples, unroll, last):
        grouped = []
        for comp in range(2):
            even = disp[it, comp, pl.ds(0, pairs, stride=2), :]
            odd = disp[it, comp, pl.ds(1, pairs, stride=2), :]
            grouped.append(jnp.concatenate(halves(even, odd, low_half), axis=0))
        for comp in range(2):
            nearest = jnp.floor(grouped[comp] + 0.5)
            f = grouped[comp] - nearest
            at_w = 6 * comp
            weights[at_w] = 0.5 * (0.5 - f) * (0.5 - f)
            weights[at_w + 1] = 0.75 - f * f
            weights[at_w + 2] = 0.5 * (0.5 + f) * (0.5 + f)
            weights[at_w + 3] = f - 0.5
            weights[at_w + 4] = -2.0 * f
            weights[at_w + 5] = 0.5 + f
            if comp == 0:
                weights[12] = nearest + REACH + second_row
            else:
                weights[13] = nearest + position

        place = lax.broadcasted_iota(jnp.int32, (128, 128), 0).astype(F32).astype(BF16)
        one_bf, zero_bf = jnp.ones((128, 128), BF16), jnp.zeros((128, 128), BF16)

        def sample(index, carry):
            half = index // triples
            triple = lax.rem(index, triples)
            first_group = half * pairs + start + triple * 3
            columns = []
            for j in range(2):
                target = weights[13, pl.ds(first_group + j, 1), :]
                for b in range(3):
                    hit = place == jnp.broadcast_to((target + (b - 1)).astype(BF16), (128, 128))
                    columns.append(jnp.where(hit, one_bf, zero_bf))
            onehot = jnp.concatenate(columns, axis=1)
            begin = (start - first_pair) * 16 + triple * 48
            window = lhs[half, pl.ds(pl.multiple_of(begin, 16), 304), :]
            picked = dot(window, jnp.concatenate([onehot, onehot], axis=0))
            target = weights[13, pl.ds(first_group + 2, 1), :]
            lane_of = [
                jnp.broadcast_to((target + (b - 1)).astype(jnp.int32), (8, 128)) for b in range(3)
            ]

            def column_tap(j, k, b):
                if j < 2:
                    n = 3 * j + b
                    return picked[(2 * j + k) * 8 : (2 * j + k) * 8 + 8, n * 128 : n * 128 + 128]
                row = lhs_f32[half, pl.ds(pl.multiple_of(begin + 32 + k * 8, 8), 8), :]
                return jnp.take_along_axis(row, lane_of[b], axis=1, mode="promise_in_bounds")

            for j in range(3):
                group = first_group + j

                def weight(k):
                    return jnp.broadcast_to(weights[k, pl.ds(group, 1), :], (8, 128))

                offset = weight(12)
                masks = []
                for shift in (17, 8, 4, 2, 1, 1):
                    mask = offset >= shift
                    masks.append(mask)
                    offset = jnp.where(mask, offset - shift, offset)
                taps_at = []
                for b in range(3):
                    rows = [column_tap(j, k, b) for k in range(36)]
                    for shift, mask, count in zip(
                        (17, 8, 4, 2, 1, 1), masks, (19, 11, 7, 5, 4, 3)
                    ):
                        rows = [jnp.where(mask, rows[k + shift], rows[k]) for k in range(count)]
                    taps_at.append(rows)
                warped = slope_row = slope_col = None
                w_row, dw_row = [weight(a) for a in range(3)], [weight(3 + a) for a in range(3)]
                for b in range(3):
                    along = sum(w_row[a] * taps_at[b][a] for a in range(3))
                    slant = sum(dw_row[a] * taps_at[b][a] for a in range(3))
                    w, dw = weight(6 + b), weight(9 + b)
                    terms = (w * along, w * slant, dw * along)
                    if b == 0:
                        warped, slope_row, slope_col = terms
                    else:
                        warped += terms[0]
                        slope_row += terms[1]
                        slope_col += terms[2]
                mismatch = warped - fixed_embed[group]
                data[0, pl.ds(group, 1), :] = jnp.sum(mismatch * slope_row, axis=0, keepdims=True)
                data[1, pl.ds(group, 1), :] = jnp.sum(mismatch * slope_col, axis=0, keepdims=True)
            return carry

        lax.fori_loop(0, 2 * triples, sample, 0, unroll=unroll)

        for side in range(2):

            @pl.when(present(WEST_EAST[side]))
            def _():
                disp_copy(it, side).wait_recv()

        lane = lanes((ext_rows, tile_cols))
        one = jnp.where(it == 0, 1 / (1 - 0.9), jnp.where(it == 1, 1 / (1 - 0.9**2), 1 / (1 - 0.9**3)))
        two = jnp.where(
            it == 0, 1 / (1 - 0.999), jnp.where(it == 1, 1 / (1 - 0.999**2), 1 / (1 - 0.999**3))
        )
        for comp in range(2):
            even, odd = halves(data[comp, 0:pairs, :], data[comp, pairs : 2 * pairs, :], low_half)
            unpaired[comp, pl.ds(0, pairs, stride=2), :] = even
            unpaired[comp, pl.ds(1, pairs, stride=2), :] = odd
            sampled = unpaired[comp] * (2.0 / CH)
            d = disp[it, comp]
            north = pltpu.roll(d, 1, 0)
            south = pltpu.roll(d, ext_rows - 1, 0)
            west = pltpu.roll(
                jnp.where(lane == tile_cols - 1, edge_col[it, 0, comp], d), 1, 1
            )
            east = pltpu.roll(
                jnp.where(lane == 0, edge_col[it, 1, comp], d), tile_cols - 1, 1
            )
            squashed = d * (1.0 / REACH)
            gradient = (
                sampled + 2.0 * stiffness * (4.0 * d - (south + north + east + west))
            ) * (1.0 - squashed * squashed)
            m1 = 0.9 * first_moment[comp] + 0.1 * gradient
            m2 = 0.999 * second_moment[comp] + 0.001 * gradient * gradient
            first_moment[comp] = m1
            second_moment[comp] = m2
            new = raw[comp] - step_size * (m1 * one) / (jnp.sqrt(m2 * two) + adam_epsilon)
            raw[comp] = new

            if not last:
                disp[it + 1, comp] = jnp.where(in_section, REACH * jnp.tanh(new / REACH), 0.0)

        if not last:
            send_disp(it + 1)

    def early(it, carry):
        step(it, first_pair, (tile_rows + 2 * EXTRA) // 6, 4, False)
        return carry

    lax.fori_loop(0, ITERS - 1, early, 0)
    step(ITERS - 1, first_pair, (tile_rows + 2 * EXTRA) // 6, 4, True)
    own_rows = slice(HALO, HALO + tile_rows)
    out_ref[...] = raw[:, own_rows, :] - field_ref[:, own_rows, :]
    for i, j in AROUND:

        @pl.when(present((-i, -j)))
        def _():
            for copy in image_copies(3 * (i + 1) + j + 1):
                copy.wait_send()

    for side in range(2):

        @pl.when(present(NORTH_SOUTH[1 - side]))
        def _():
            field_copy(side).wait_send()

        @pl.when(present(WEST_EAST[1 - side]))
        def _():
            for it in range(ITERS):
                disp_copy(it, side).wait_send()


def local(rows_of_mesh, cols_of_mesh, fixed, moving, field, w1, b1, w2):
    tile_rows, tile_cols = fixed.shape
    vmem = pl.BlockSpec(memory_space=pltpu.VMEM)
    tile = (tile_rows, tile_cols)
    ext = tile_rows + 2 * HALO
    return pl.pallas_call(
        functools.partial(kernel, rows_of_mesh, cols_of_mesh),
        out_shape=jax.ShapeDtypeStruct(field.shape, F32),
        in_specs=[pl.BlockSpec(memory_space=pltpu.HBM)] * 6,
        out_specs=vmem,
        scratch_shapes=[
            pltpu.VMEM((2, ext, tile_cols), F32),
            pltpu.VMEM(w1.shape, F32),
            pltpu.SMEM(b1.shape, F32),
            pltpu.VMEM(w2.shape, F32),
            pltpu.VMEM((2,) + tile, BF16),
            pltpu.VMEM((9, 2) + tile, BF16),
            pltpu.VMEM((3, 80, 256), F32),
            pltpu.VMEM((3 * SLAB * 8, 256), BF16),
            pltpu.VMEM((2, 70 * 8, 256), BF16),
            pltpu.VMEM((2, 70 * 8, 128), F32),
            pltpu.VMEM((ext, 8, 128), F32),
            pltpu.VMEM((ITERS, 2, ext, tile_cols), F32),
            pltpu.VMEM((ITERS, 2, 2, ext, tile_cols), F32),
            pltpu.VMEM((2, ext, tile_cols), F32),
            pltpu.VMEM((2, ext, tile_cols), F32),
            pltpu.VMEM((2, ext, tile_cols), F32),
            pltpu.VMEM((14, ext, 128), F32),
            pltpu.VMEM((2, ext, 128), F32),
            pltpu.VMEM((2, ext, 128), F32),
            pltpu.SemaphoreType.DMA((1, 9)),
            pltpu.SemaphoreType.DMA((1, 9)),
            pltpu.SemaphoreType.DMA((2,)),
            pltpu.SemaphoreType.DMA((2,)),
            pltpu.SemaphoreType.DMA((ITERS, 2)),
            pltpu.SemaphoreType.DMA((ITERS, 2)),
            pltpu.SemaphoreType.DMA((6,)),
        ],
        compiler_params=pltpu.CompilerParams(
            collective_id=0, has_side_effects=True, vmem_limit_bytes=32 << 20
        ),
        name="refine",
    )(*(pltpu.with_memory_space_constraint(x, pltpu.HBM) for x in (fixed, moving, field, w1, b1, w2)))


def solution(mesh):
    return jax.shard_map(
        functools.partial(local, mesh.shape["row"], mesh.shape["col"]),
        mesh=mesh,
        in_specs=(P("row", "col"), P("row", "col"), P(None, "row", "col"), P(), P(), P()),
        out_specs=P(None, "row", "col"),
        check_vma=False,
    )
```

```python
import functools

import jax
import jax.numpy as jnp
from jax import lax
from jax.experimental import pallas as pl
from jax.experimental.pallas import tpu as pltpu
from jax.sharding import PartitionSpec as P

REACH = 16
ITERS = 3
CH = 8

stiffness = 0.01
step_size = 0.5
adam_epsilon = 0.01

F32 = jnp.float32
BF16 = jnp.bfloat16
MESH = pl.DeviceIdType.MESH
AROUND = [(-1, -1), (-1, 1), (1, -1), (1, 1), (-1, 0), (1, 0), (0, -1), (0, 1)]
NORTH_SOUTH = [(-1, 0), (1, 0)]
WEST_EAST = [(0, -1), (0, 1)]
HALO = 8
EXTRA = 2
SLAB = 14


def lanes(shape):
    return lax.broadcasted_iota(jnp.int32, shape, len(shape) - 1)


def split(x):
    high = x.astype(BF16)
    return high, (x - high.astype(F32)).astype(BF16)


def dot(a, b):
    return lax.dot_general(a, b, (((1,), (0,)), ((), ())), preferred_element_type=F32)


def kernel(
    rows_of_mesh,
    cols_of_mesh,
    fixed_hbm,
    moving_hbm,
    field_hbm,
    w1_hbm,
    b1_hbm,
    w2_hbm,
    out_ref,
    field_ref,
    w1_ref,
    b1_ref,
    w2_ref,
    own,
    around,
    shifted,
    toeplitz,
    lhs,
    lhs_f32,
    fixed_embed,
    disp,
    edge_col,
    raw,
    first_moment,
    second_moment,
    weights,
    products,
    unpaired,
    image_send,
    image_recv,
    field_send,
    field_recv,
    disp_send,
    disp_recv,
    load_sem,
):
    me_row, me_col = lax.axis_index("row"), lax.axis_index("col")
    tile_rows, tile_cols = fixed_hbm.shape
    ext_rows = tile_rows + 2 * HALO

    def at(offset):
        return me_row + offset[0], me_col + offset[1]

    def present(offset):
        row, col = at(offset)
        return (row >= 0) & (row < rows_of_mesh) & (col >= 0) & (col < cols_of_mesh)

    barrier = pltpu.get_barrier_semaphore()
    for offset in AROUND:

        @pl.when(present(offset))
        def _():
            pl.semaphore_signal(barrier, inc=1, device_id=at(offset), device_id_type=MESH)

    loads = [
        pltpu.make_async_copy(src, dst, load_sem.at[i])
        for i, (src, dst) in enumerate(
            [
                (field_hbm, field_ref.at[:, pl.ds(HALO, tile_rows), :]),
                (moving_hbm, own.at[1]),
                (fixed_hbm, own.at[0]),
                (w2_hbm, w2_ref),
                (w1_hbm, w1_ref),
                (b1_hbm, b1_ref),
            ]
        )
    ]
    for load in loads:
        load.start()
    for offset in AROUND:
        slot = 3 * (offset[0] + 1) + offset[1] + 1

        @pl.when(jnp.logical_not(present(offset)))
        def _():
            around[slot] = jnp.zeros(around.shape[1:], BF16)

    for side in range(2):

        @pl.when(jnp.logical_not(present(NORTH_SOUTH[side])))
        def _():
            at_row = side * (HALO + tile_rows)
            field_ref[:, at_row : at_row + HALO, :] = jnp.zeros((2, HALO, tile_cols), F32)

        @pl.when(jnp.logical_not(present(WEST_EAST[side])))
        def _():
            edge_col[:, side] = jnp.zeros((ITERS,) + edge_col.shape[2:], F32)

    products[...] = jnp.zeros_like(products)
    first_moment[...] = jnp.zeros_like(first_moment)
    second_moment[...] = jnp.zeros_like(second_moment)

    def image_copies(slot):
        i, j = 1 - slot // 3, 1 - slot % 3
        return [
            pltpu.make_async_remote_copy(
                src_ref=own,
                dst_ref=around.at[slot],
                send_sem=image_send.at[0, slot],
                recv_sem=image_recv.at[0, slot],
                device_id=at((i, j)),
                device_id_type=MESH,
            )
        ]

    def field_copy(side):
        i, _ = NORTH_SOUTH[side]
        return pltpu.make_async_remote_copy(
            src_ref=field_hbm.at[:, pl.ds((tile_rows - HALO) * (1 - side), HALO), :],
            dst_ref=field_ref.at[:, pl.ds((HALO + tile_rows) * side, HALO), :],
            send_sem=field_send.at[side],
            recv_sem=field_recv.at[side],
            device_id=at((-i, 0)),
            device_id_type=MESH,
        )

    def disp_copy(step, side):
        _, j = WEST_EAST[side]
        return pltpu.make_async_remote_copy(
            src_ref=disp.at[step],
            dst_ref=edge_col.at[step, side],
            send_sem=disp_send.at[step, side],
            recv_sem=disp_recv.at[step, side],
            device_id=at((0, -j)),
            device_id_type=MESH,
        )

    def send_disp(step):
        for side in range(2):

            @pl.when(present(WEST_EAST[1 - side]))
            def _():
                disp_copy(step, side).start()

    for load in loads:
        load.wait()

    rows_near = 1 + (me_row > 0).astype(jnp.int32) + (me_row < rows_of_mesh - 1).astype(jnp.int32)
    cols_near = 1 + (me_col > 0).astype(jnp.int32) + (me_col < cols_of_mesh - 1).astype(jnp.int32)
    pl.semaphore_wait(barrier, rows_near * cols_near - 1)
    for i, j in AROUND:

        @pl.when(present((-i, -j)))
        def _():
            for copy in image_copies(3 * (i + 1) + j + 1):
                copy.start()

    for side in range(2):

        @pl.when(present(NORTH_SOUTH[1 - side]))
        def _():
            field_copy(side).start()

    sub64 = lax.broadcasted_iota(jnp.int32, (64, 128), 0)
    lane64 = lanes((64, 128))
    w2 = w2_ref[...].reshape(64, 9)
    for tap_col in range(3):
        spread = jnp.zeros((64, 128), F32)
        for tap_row in range(3):
            column = w2[:, 3 * tap_row + tap_col : 3 * tap_row + tap_col + 1]
            spread = jnp.where(
                lane64 == tap_row * 8 + (sub64 & 7), jnp.broadcast_to(column, (64, 128)), spread
            )
        base = jnp.sum(spread.reshape(8, 8, 128), axis=1)
        block = jnp.concatenate(
            [base if i == 0 else pltpu.roll(base, 8 * i, 1) for i in range(SLAB)], axis=0
        )
        high, low = split(block)
        at_row = tap_col * SLAB * 8
        toeplitz[at_row : at_row + SLAB * 8, 0:128] = high
        toeplitz[at_row : at_row + SLAB * 8, 128:256] = low
    w1 = w1_ref[...]
    taps = [jnp.broadcast_to(w1[:, k : k + 1], (8, 256)) for k in range(9)]
    sub8 = lax.broadcasted_iota(jnp.int32, (8, 256), 0)
    bias = jnp.zeros((8, 256), F32)
    for ch in range(CH):
        bias = jnp.where(sub8 == ch, b1_ref[ch], bias)

    for side in range(2):

        @pl.when(present(NORTH_SOUTH[side]))
        def _():
            field_copy(side).wait_recv()

    full_rows, full_cols = rows_of_mesh * tile_rows, cols_of_mesh * tile_cols
    row_ext = me_row * tile_rows - HALO + lax.broadcasted_iota(
        jnp.int32, (ext_rows, tile_cols), 0
    )
    in_section = (row_ext >= 0) & (row_ext < full_rows)
    for comp in range(2):
        raw[comp] = field_ref[comp]
        disp[0, comp] = jnp.where(in_section, REACH * jnp.tanh(field_ref[comp] / REACH), 0.0)
    send_disp(0)

    for i, j in AROUND:

        @pl.when(present((i, j)))
        def _():
            for copy in image_copies(3 * (i + 1) + j + 1):
                copy.wait_recv()

    lane_tile = lanes((80, 128))

    def encode(which, first_lane, first_row, row_margin, margin, slabs, store):
        def tile(slot):
            if slot == 4:
                return own[which].astype(F32)
            return around[slot, which].astype(F32)

        bands = []
        for col in range(3):
            bands.append(
                jnp.concatenate(
                    [tile(col)[8:, :], tile(3 + col), tile(6 + col)[: tile_rows - 8, :]], axis=0
                )
            )
        for tap_col in range(3):
            start = first_lane + tap_col
            if start == 128:
                left, right = bands[1], bands[2]
            else:
                turned = [pltpu.roll(x, 128 - start, 1) for x in bands]
                inside = lane_tile < 128 - start
                left = jnp.where(inside, turned[0], turned[1])
                right = jnp.where(inside, turned[1], turned[2])
            shifted[tap_col, :, 0:128] = left
            shifted[tap_col, :, 128:256] = right

        lane8 = lanes((8, 256))
        col8 = me_col * tile_cols + lane8 - (margin + 1)
        col_in = (col8 >= 0) & (col8 < full_cols)
        lane_e = lanes((SLAB * 8, 256))
        row_e = lax.broadcasted_iota(jnp.int32, (SLAB * 8, 256), 0) // 8
        col_e = me_col * tile_cols + lane_e - margin
        ok_col = (col_e >= 0) & (col_e < full_cols) & (lane_e < tile_cols + 2 * margin)

        for slab in slabs:
            hidden = []
            pixels = {}
            for i in range(SLAB + 4):
                for tap_col in range(3):
                    pixel = shifted[tap_col, pl.ds(first_row + slab + i, 1), :]
                    pixels[i, tap_col] = jnp.broadcast_to(pixel, (8, 256))
            for i in range(SLAB + 2):
                h = bias
                for tap in range(9):
                    h = h + taps[tap] * pixels[i + tap // 3, tap % 3]
                row = me_row * tile_rows + (slab + i - row_margin - 1)
                row_ok = (row >= 0) & (row < full_rows)
                row_factor = jnp.where(row_ok, 1.0, 0.0).astype(F32)
                hidden.append(jnp.where(col_in, jnp.maximum(h, 0.0) * row_factor, 0.0))
            high, low = split(jnp.concatenate(hidden, axis=0))
            t_high, t_low = toeplitz[:, 0:128], toeplitz[:, 128:256]
            product = dot(
                jnp.concatenate([t_high, t_high], axis=1), jnp.concatenate([high, low], axis=0)
            ) + dot(t_low, high)
            n = SLAB * 8
            embed = (
                product[0:n]
                + pltpu.roll(product[n : 2 * n], 255, 1)
                + pltpu.roll(product[2 * n : 3 * n], 254, 1)
            )
            row_abs = me_row * tile_rows + row_e + (slab - row_margin)
            embed = jnp.where(ok_col & (row_abs >= 0) & (row_abs < full_rows), embed, 0.0)
            store(slab, embed)

    def halves(even, odd, low_half):
        axis = even.ndim - 1
        return (
            jnp.where(low_half, even, pltpu.roll(odd, 64, axis)),
            jnp.where(low_half, pltpu.roll(even, 64, axis), odd),
        )

    low8 = lanes((8, 128)) < 64
    pairs = ext_rows // 2
    first_pair = (HALO - EXTRA) // 2

    def store_fixed(slab, embed):
        for pair in range(SLAB // 2):
            even = embed[pair * 16 : pair * 16 + 8, 0:128]
            odd = embed[pair * 16 + 8 : pair * 16 + 16, 0:128]
            left, right = halves(even, odd, low8)
            at_pair = first_pair + slab // 2 + pair
            fixed_embed[at_pair] = left
            fixed_embed[pairs + at_pair] = right

    low_e = lanes((SLAB * 8, 128)) < 64

    def store_moving(slab, embed):
        a, b = embed[:, 0:128], embed[:, 128:256]
        middle = jnp.where(low_e, pltpu.roll(a, 64, 1), pltpu.roll(b, 64, 1))
        for half, part in enumerate((a, middle)):
            lhs_f32[half, slab * 8 : (slab + SLAB) * 8, :] = part
            high, low = split(part)
            lhs[half, slab * 8 : (slab + SLAB) * 8, 0:128] = high
            lhs[half, slab * 8 : (slab + SLAB) * 8, 128:256] = low

    encode(0, 126, 24 - EXTRA - 2, EXTRA, 0, (0, 14, 22), store_fixed)
    encode(
        1, 109, 24 - EXTRA - REACH - 3, EXTRA + REACH + 1, REACH + 1, (0, 14, 28, 42, 56), store_moving
    )

    low_half = lanes((pairs, 128)) < 64
    lane_g = lanes((2 * pairs, 128))
    position = (lane_g & 63).astype(F32) + (REACH + 1)
    second_row = jnp.where(lane_g >= 64, 1.0, 0.0).astype(F32)

    def step(it, start, triples, unroll, last):
        grouped = []
        for comp in range(2):
            even = disp[it, comp, pl.ds(0, pairs, stride=2), :]
            odd = disp[it, comp, pl.ds(1, pairs, stride=2), :]
            grouped.append(jnp.concatenate(halves(even, odd, low_half), axis=0))
        for comp in range(2):
            nearest = jnp.floor(grouped[comp] + 0.5)
            f = grouped[comp] - nearest
            at_w = 6 * comp
            weights[at_w] = 0.5 * (0.5 - f) * (0.5 - f)
            weights[at_w + 1] = 0.75 - f * f
            weights[at_w + 2] = 0.5 * (0.5 + f) * (0.5 + f)
            weights[at_w + 3] = f - 0.5
            weights[at_w + 4] = -2.0 * f
            weights[at_w + 5] = 0.5 + f
            if comp == 0:
                weights[12] = nearest + REACH + second_row
            else:
                weights[13] = nearest + position

        place = lax.broadcasted_iota(jnp.int32, (128, 128), 0).astype(F32).astype(BF16)
        one_bf, zero_bf = jnp.ones((128, 128), BF16), jnp.zeros((128, 128), BF16)

        def sample(index, carry):
            half = index // triples
            triple = lax.rem(index, triples)
            first_group = half * pairs + start + triple * 3
            columns = []
            for j in range(2):
                target = weights[13, pl.ds(first_group + j, 1), :]
                for b in range(3):
                    hit = place == jnp.broadcast_to((target + (b - 1)).astype(BF16), (128, 128))
                    columns.append(jnp.where(hit, one_bf, zero_bf))
            onehot = jnp.concatenate(columns, axis=1)
            begin = (start - first_pair) * 16 + triple * 48
            window = lhs[half, pl.ds(pl.multiple_of(begin, 16), 304), :]
            picked = dot(window, jnp.concatenate([onehot, onehot], axis=0))
            target = weights[13, pl.ds(first_group + 2, 1), :]
            lane_of = [
                jnp.broadcast_to((target + (b - 1)).astype(jnp.int32), (8, 128)) for b in range(3)
            ]

            def column_tap(j, k, b):
                if j < 2:
                    n = 3 * j + b
                    return picked[(2 * j + k) * 8 : (2 * j + k) * 8 + 8, n * 128 : n * 128 + 128]
                row = lhs_f32[half, pl.ds(pl.multiple_of(begin + 32 + k * 8, 8), 8), :]
                return jnp.take_along_axis(row, lane_of[b], axis=1, mode="promise_in_bounds")

            for j in range(3):
                group = first_group + j

                def weight(k):
                    return jnp.broadcast_to(weights[k, pl.ds(group, 1), :], (8, 128))

                offset = weight(12)
                masks = []
                for shift in (17, 8, 4, 2, 1, 1):
                    mask = offset >= shift
                    masks.append(mask)
                    offset = jnp.where(mask, offset - shift, offset)
                taps_at = []
                for b in range(3):
                    rows = [column_tap(j, k, b) for k in range(36)]
                    for shift, mask, count in zip(
                        (17, 8, 4, 2, 1, 1), masks, (19, 11, 7, 5, 4, 3)
                    ):
                        rows = [jnp.where(mask, rows[k + shift], rows[k]) for k in range(count)]
                    taps_at.append(rows)
                warped = slope_row = slope_col = None
                w_row, dw_row = [weight(a) for a in range(3)], [weight(3 + a) for a in range(3)]
                for b in range(3):
                    along = sum(w_row[a] * taps_at[b][a] for a in range(3))
                    slant = sum(dw_row[a] * taps_at[b][a] for a in range(3))
                    w, dw = weight(6 + b), weight(9 + b)
                    terms = (w * along, w * slant, dw * along)
                    if b == 0:
                        warped, slope_row, slope_col = terms
                    else:
                        warped += terms[0]
                        slope_row += terms[1]
                        slope_col += terms[2]
                mismatch = warped - fixed_embed[group]
                at_group = pl.ds(pl.multiple_of(group * CH, CH), CH)
                products[0, at_group, :] = mismatch * slope_row
                products[1, at_group, :] = mismatch * slope_col
            return carry

        lax.fori_loop(0, 2 * triples, sample, 0, unroll=unroll)

        for side in range(2):

            @pl.when(present(WEST_EAST[side]))
            def _():
                disp_copy(it, side).wait_recv()

        lane = lanes((ext_rows, tile_cols))
        one = jnp.where(it == 0, 1 / (1 - 0.9), jnp.where(it == 1, 1 / (1 - 0.9**2), 1 / (1 - 0.9**3)))
        two = jnp.where(
            it == 0, 1 / (1 - 0.999), jnp.where(it == 1, 1 / (1 - 0.999**2), 1 / (1 - 0.999**3))
        )
        for comp in range(2):
            summed = sum(products[comp, pl.ds(ch, 2 * pairs, stride=CH), :] for ch in range(CH))
            even, odd = halves(summed[0:pairs], summed[pairs : 2 * pairs], low_half)
            unpaired[comp, pl.ds(0, pairs, stride=2), :] = even
            unpaired[comp, pl.ds(1, pairs, stride=2), :] = odd
            sampled = unpaired[comp] * (2.0 / CH)
            d = disp[it, comp]
            north = pltpu.roll(d, 1, 0)
            south = pltpu.roll(d, ext_rows - 1, 0)
            west = pltpu.roll(
                jnp.where(lane == tile_cols - 1, edge_col[it, 0, comp], d), 1, 1
            )
            east = pltpu.roll(
                jnp.where(lane == 0, edge_col[it, 1, comp], d), tile_cols - 1, 1
            )
            squashed = d * (1.0 / REACH)
            gradient = (
                sampled + 2.0 * stiffness * (4.0 * d - (south + north + east + west))
            ) * (1.0 - squashed * squashed)
            m1 = 0.9 * first_moment[comp] + 0.1 * gradient
            m2 = 0.999 * second_moment[comp] + 0.001 * gradient * gradient
            first_moment[comp] = m1
            second_moment[comp] = m2
            new = raw[comp] - step_size * (m1 * one) / (jnp.sqrt(m2 * two) + adam_epsilon)
            raw[comp] = new

            if not last:
                disp[it + 1, comp] = jnp.where(in_section, REACH * jnp.tanh(new / REACH), 0.0)

        if not last:
            send_disp(it + 1)

    def early(it, carry):
        step(it, first_pair, (tile_rows + 2 * EXTRA) // 6, 12, False)
        return carry

    lax.fori_loop(0, ITERS - 1, early, 0)
    step(ITERS - 1, first_pair, (tile_rows + 2 * EXTRA) // 6, 12, True)
    own_rows = slice(HALO, HALO + tile_rows)
    out_ref[...] = raw[:, own_rows, :] - field_ref[:, own_rows, :]
    for i, j in AROUND:

        @pl.when(present((-i, -j)))
        def _():
            for copy in image_copies(3 * (i + 1) + j + 1):
                copy.wait_send()

    for side in range(2):

        @pl.when(present(NORTH_SOUTH[1 - side]))
        def _():
            field_copy(side).wait_send()

        @pl.when(present(WEST_EAST[1 - side]))
        def _():
            for it in range(ITERS):
                disp_copy(it, side).wait_send()


def local(rows_of_mesh, cols_of_mesh, fixed, moving, field, w1, b1, w2):
    tile_rows, tile_cols = fixed.shape
    vmem = pl.BlockSpec(memory_space=pltpu.VMEM)
    tile = (tile_rows, tile_cols)
    ext = tile_rows + 2 * HALO
    return pl.pallas_call(
        functools.partial(kernel, rows_of_mesh, cols_of_mesh),
        out_shape=jax.ShapeDtypeStruct(field.shape, F32),
        in_specs=[pl.BlockSpec(memory_space=pltpu.HBM)] * 6,
        out_specs=vmem,
        scratch_shapes=[
            pltpu.VMEM((2, ext, tile_cols), F32),
            pltpu.VMEM(w1.shape, F32),
            pltpu.SMEM(b1.shape, F32),
            pltpu.VMEM(w2.shape, F32),
            pltpu.VMEM((2,) + tile, BF16),
            pltpu.VMEM((9, 2) + tile, BF16),
            pltpu.VMEM((3, 80, 256), F32),
            pltpu.VMEM((3 * SLAB * 8, 256), BF16),
            pltpu.VMEM((2, 70 * 8, 256), BF16),
            pltpu.VMEM((2, 70 * 8, 128), F32),
            pltpu.VMEM((ext, 8, 128), F32),
            pltpu.VMEM((ITERS, 2, ext, tile_cols), F32),
            pltpu.VMEM((ITERS, 2, 2, ext, tile_cols), F32),
            pltpu.VMEM((2, ext, tile_cols), F32),
            pltpu.VMEM((2, ext, tile_cols), F32),
            pltpu.VMEM((2, ext, tile_cols), F32),
            pltpu.VMEM((14, ext, 128), F32),
            pltpu.VMEM((2, ext * CH, 128), F32),
            pltpu.VMEM((2, ext, 128), F32),
            pltpu.SemaphoreType.DMA((1, 9)),
            pltpu.SemaphoreType.DMA((1, 9)),
            pltpu.SemaphoreType.DMA((2,)),
            pltpu.SemaphoreType.DMA((2,)),
            pltpu.SemaphoreType.DMA((ITERS, 2)),
            pltpu.SemaphoreType.DMA((ITERS, 2)),
            pltpu.SemaphoreType.DMA((6,)),
        ],
        compiler_params=pltpu.CompilerParams(
            collective_id=0, has_side_effects=True, vmem_limit_bytes=32 << 20
        ),
        name="refine",
    )(*(pltpu.with_memory_space_constraint(x, pltpu.HBM) for x in (fixed, moving, field, w1, b1, w2)))


def solution(mesh):
    return jax.shard_map(
        functools.partial(local, mesh.shape["row"], mesh.shape["col"]),
        mesh=mesh,
        in_specs=(P("row", "col"), P("row", "col"), P(None, "row", "col"), P(), P(), P()),
        out_specs=P(None, "row", "col"),
        check_vma=False,
    )
```

```python
import functools

import jax
import jax.numpy as jnp
from jax import lax
from jax.experimental import pallas as pl
from jax.experimental.pallas import tpu as pltpu
from jax.sharding import PartitionSpec as P

REACH = 16
ITERS = 3
CH = 8

stiffness = 0.01
step_size = 0.5
adam_epsilon = 0.01

F32 = jnp.float32
BF16 = jnp.bfloat16
MESH = pl.DeviceIdType.MESH
AROUND = [(-1, -1), (-1, 1), (1, -1), (1, 1), (-1, 0), (1, 0), (0, -1), (0, 1)]
NORTH_SOUTH = [(-1, 0), (1, 0)]
WEST_EAST = [(0, -1), (0, 1)]
HALO = 8
EXTRA = 2
SLAB = 14


def lanes(shape):
    return lax.broadcasted_iota(jnp.int32, shape, len(shape) - 1)


def split(x):
    high = x.astype(BF16)
    return high, (x - high.astype(F32)).astype(BF16)


def dot(a, b):
    return lax.dot_general(a, b, (((1,), (0,)), ((), ())), preferred_element_type=F32)


def kernel(
    rows_of_mesh,
    cols_of_mesh,
    fixed_hbm,
    moving_hbm,
    field_hbm,
    w1_hbm,
    b1_hbm,
    w2_hbm,
    out_ref,
    field_ref,
    w1_ref,
    b1_ref,
    w2_ref,
    own,
    around,
    shifted,
    toeplitz,
    lhs,
    lhs_f32,
    fixed_embed,
    disp,
    edges,
    edge_col,
    raw,
    first_moment,
    second_moment,
    weights,
    products,
    unpaired,
    image_send,
    image_recv,
    field_send,
    field_recv,
    disp_send,
    disp_recv,
    load_sem,
):
    me_row, me_col = lax.axis_index("row"), lax.axis_index("col")
    tile_rows, tile_cols = fixed_hbm.shape
    ext_rows = tile_rows + 2 * HALO

    def at(offset):
        return me_row + offset[0], me_col + offset[1]

    def present(offset):
        row, col = at(offset)
        return (row >= 0) & (row < rows_of_mesh) & (col >= 0) & (col < cols_of_mesh)

    barrier = pltpu.get_barrier_semaphore()
    for offset in AROUND:

        @pl.when(present(offset))
        def _():
            pl.semaphore_signal(barrier, inc=1, device_id=at(offset), device_id_type=MESH)

    loads = [
        pltpu.make_async_copy(src, dst, load_sem.at[i])
        for i, (src, dst) in enumerate(
            [
                (field_hbm, field_ref.at[:, pl.ds(HALO, tile_rows), :]),
                (moving_hbm, own.at[1]),
                (fixed_hbm, own.at[0]),
                (w2_hbm, w2_ref),
                (w1_hbm, w1_ref),
                (b1_hbm, b1_ref),
            ]
        )
    ]
    for load in loads:
        load.start()
    for offset in AROUND:
        slot = 3 * (offset[0] + 1) + offset[1] + 1

        @pl.when(jnp.logical_not(present(offset)))
        def _():
            around[slot] = jnp.zeros(around.shape[1:], BF16)

    for side in range(2):

        @pl.when(jnp.logical_not(present(NORTH_SOUTH[side])))
        def _():
            at_row = side * (HALO + tile_rows)
            field_ref[:, at_row : at_row + HALO, :] = jnp.zeros((2, HALO, tile_cols), F32)

        @pl.when(jnp.logical_not(present(WEST_EAST[side])))
        def _():
            edge_col[:, side] = jnp.zeros((ITERS,) + edge_col.shape[2:], F32)

    products[...] = jnp.zeros_like(products)
    first_moment[...] = jnp.zeros_like(first_moment)
    second_moment[...] = jnp.zeros_like(second_moment)

    def image_copies(slot):
        i, j = 1 - slot // 3, 1 - slot % 3
        return [
            pltpu.make_async_remote_copy(
                src_ref=own,
                dst_ref=around.at[slot],
                send_sem=image_send.at[0, slot],
                recv_sem=image_recv.at[0, slot],
                device_id=at((i, j)),
                device_id_type=MESH,
            )
        ]

    def field_copy(side):
        i, _ = NORTH_SOUTH[side]
        return pltpu.make_async_remote_copy(
            src_ref=field_hbm.at[:, pl.ds((tile_rows - HALO) * (1 - side), HALO), :],
            dst_ref=field_ref.at[:, pl.ds((HALO + tile_rows) * side, HALO), :],
            send_sem=field_send.at[side],
            recv_sem=field_recv.at[side],
            device_id=at((-i, 0)),
            device_id_type=MESH,
        )

    def disp_copy(step, side):
        _, j = WEST_EAST[side]
        return pltpu.make_async_remote_copy(
            src_ref=edges.at[step],
            dst_ref=edge_col.at[step, side],
            send_sem=disp_send.at[step, side],
            recv_sem=disp_recv.at[step, side],
            device_id=at((0, -j)),
            device_id_type=MESH,
        )

    lane_edge = lanes((8, 128))
    blocks = ext_rows // 8

    def send_disp(step):
        first, last = jnp.zeros((8, 128), F32), jnp.zeros((8, 128), F32)
        for n in range(2 * blocks):
            at_row = n % blocks * 8
            block = disp[step, n // blocks, at_row : at_row + 8, :]
            first = jnp.where(lane_edge == n, pltpu.roll(block, n, 1) if n else block, first)
            last = jnp.where(lane_edge == n, pltpu.roll(block, n + 1, 1), last)
        edges[step, 0:8, :] = first
        edges[step, 8:16, :] = last
        for side in range(2):

            @pl.when(present(WEST_EAST[1 - side]))
            def _():
                disp_copy(step, side).start()

    for load in loads:
        load.wait()

    rows_near = 1 + (me_row > 0).astype(jnp.int32) + (me_row < rows_of_mesh - 1).astype(jnp.int32)
    cols_near = 1 + (me_col > 0).astype(jnp.int32) + (me_col < cols_of_mesh - 1).astype(jnp.int32)
    pl.semaphore_wait(barrier, rows_near * cols_near - 1)
    for i, j in AROUND:

        @pl.when(present((-i, -j)))
        def _():
            for copy in image_copies(3 * (i + 1) + j + 1):
                copy.start()

    for side in range(2):

        @pl.when(present(NORTH_SOUTH[1 - side]))
        def _():
            field_copy(side).start()

    sub64 = lax.broadcasted_iota(jnp.int32, (64, 128), 0)
    lane64 = lanes((64, 128))
    w2 = w2_ref[...].reshape(64, 9)
    for tap_col in range(3):
        spread = jnp.zeros((64, 128), F32)
        for tap_row in range(3):
            column = w2[:, 3 * tap_row + tap_col : 3 * tap_row + tap_col + 1]
            spread = jnp.where(
                lane64 == tap_row * 8 + (sub64 & 7), jnp.broadcast_to(column, (64, 128)), spread
            )
        base = jnp.sum(spread.reshape(8, 8, 128), axis=1)
        block = jnp.concatenate(
            [base if i == 0 else pltpu.roll(base, 8 * i, 1) for i in range(SLAB)], axis=0
        )
        high, low = split(block)
        at_row = tap_col * SLAB * 8
        toeplitz[at_row : at_row + SLAB * 8, 0:128] = high
        toeplitz[at_row : at_row + SLAB * 8, 128:256] = low
    w1 = w1_ref[...]
    taps = [jnp.broadcast_to(w1[:, k : k + 1], (8, 256)) for k in range(9)]
    sub8 = lax.broadcasted_iota(jnp.int32, (8, 256), 0)
    bias = jnp.zeros((8, 256), F32)
    for ch in range(CH):
        bias = jnp.where(sub8 == ch, b1_ref[ch], bias)

    for side in range(2):

        @pl.when(present(NORTH_SOUTH[side]))
        def _():
            field_copy(side).wait_recv()

    full_rows, full_cols = rows_of_mesh * tile_rows, cols_of_mesh * tile_cols
    row_ext = me_row * tile_rows - HALO + lax.broadcasted_iota(
        jnp.int32, (ext_rows, tile_cols), 0
    )
    in_section = (row_ext >= 0) & (row_ext < full_rows)
    for comp in range(2):
        raw[comp] = field_ref[comp]
        disp[0, comp] = jnp.where(in_section, REACH * jnp.tanh(field_ref[comp] / REACH), 0.0)
    send_disp(0)

    for i, j in AROUND:

        @pl.when(present((i, j)))
        def _():
            for copy in image_copies(3 * (i + 1) + j + 1):
                copy.wait_recv()

    lane_tile = lanes((80, 128))

    def encode(which, first_lane, first_row, row_margin, margin, slabs, store):
        def tile(slot):
            if slot == 4:
                return own[which].astype(F32)
            return around[slot, which].astype(F32)

        bands = []
        for col in range(3):
            bands.append(
                jnp.concatenate(
                    [tile(col)[8:, :], tile(3 + col), tile(6 + col)[: tile_rows - 8, :]], axis=0
                )
            )
        for tap_col in range(3):
            start = first_lane + tap_col
            if start == 128:
                left, right = bands[1], bands[2]
            else:
                turned = [pltpu.roll(x, 128 - start, 1) for x in bands]
                inside = lane_tile < 128 - start
                left = jnp.where(inside, turned[0], turned[1])
                right = jnp.where(inside, turned[1], turned[2])
            shifted[tap_col, :, 0:128] = left
            shifted[tap_col, :, 128:256] = right

        lane8 = lanes((8, 256))
        col8 = me_col * tile_cols + lane8 - (margin + 1)
        col_in = (col8 >= 0) & (col8 < full_cols)
        lane_e = lanes((SLAB * 8, 256))
        row_e = lax.broadcasted_iota(jnp.int32, (SLAB * 8, 256), 0) // 8
        col_e = me_col * tile_cols + lane_e - margin
        ok_col = (col_e >= 0) & (col_e < full_cols) & (lane_e < tile_cols + 2 * margin)

        for slab in slabs:
            hidden = []
            pixels = {}
            for i in range(SLAB + 4):
                for tap_col in range(3):
                    pixel = shifted[tap_col, pl.ds(first_row + slab + i, 1), :]
                    pixels[i, tap_col] = jnp.broadcast_to(pixel, (8, 256))
            for i in range(SLAB + 2):
                h = bias
                for tap in range(9):
                    h = h + taps[tap] * pixels[i + tap // 3, tap % 3]
                row = me_row * tile_rows + (slab + i - row_margin - 1)
                row_ok = (row >= 0) & (row < full_rows)
                row_factor = jnp.where(row_ok, 1.0, 0.0).astype(F32)
                hidden.append(jnp.where(col_in, jnp.maximum(h, 0.0) * row_factor, 0.0))
            high, low = split(jnp.concatenate(hidden, axis=0))
            t_high, t_low = toeplitz[:, 0:128], toeplitz[:, 128:256]
            product = dot(
                jnp.concatenate([t_high, t_high], axis=1), jnp.concatenate([high, low], axis=0)
            ) + dot(t_low, high)
            n = SLAB * 8
            embed = (
                product[0:n]
                + pltpu.roll(product[n : 2 * n], 255, 1)
                + pltpu.roll(product[2 * n : 3 * n], 254, 1)
            )
            row_abs = me_row * tile_rows + row_e + (slab - row_margin)
            embed = jnp.where(ok_col & (row_abs >= 0) & (row_abs < full_rows), embed, 0.0)
            store(slab, embed)

    def halves(even, odd, low_half):
        axis = even.ndim - 1
        return (
            jnp.where(low_half, even, pltpu.roll(odd, 64, axis)),
            jnp.where(low_half, pltpu.roll(even, 64, axis), odd),
        )

    low8 = lanes((8, 128)) < 64
    pairs = ext_rows // 2
    first_pair = (HALO - EXTRA) // 2

    def store_fixed(slab, embed):
        for pair in range(SLAB // 2):
            even = embed[pair * 16 : pair * 16 + 8, 0:128]
            odd = embed[pair * 16 + 8 : pair * 16 + 16, 0:128]
            left, right = halves(even, odd, low8)
            at_pair = first_pair + slab // 2 + pair
            fixed_embed[at_pair] = left
            fixed_embed[pairs + at_pair] = right

    low_e = lanes((SLAB * 8, 128)) < 64

    def store_moving(slab, embed):
        a, b = embed[:, 0:128], embed[:, 128:256]
        middle = jnp.where(low_e, pltpu.roll(a, 64, 1), pltpu.roll(b, 64, 1))
        for half, part in enumerate((a, middle)):
            lhs_f32[half, slab * 8 : (slab + SLAB) * 8, :] = part
            high, low = split(part)
            lhs[half, slab * 8 : (slab + SLAB) * 8, 0:128] = high
            lhs[half, slab * 8 : (slab + SLAB) * 8, 128:256] = low

    encode(0, 126, 24 - EXTRA - 2, EXTRA, 0, (0, 14, 22), store_fixed)
    encode(
        1, 109, 24 - EXTRA - REACH - 3, EXTRA + REACH + 1, REACH + 1, (0, 14, 28, 42, 56), store_moving
    )

    low_half = lanes((pairs, 128)) < 64
    lane_g = lanes((2 * pairs, 128))
    position = (lane_g & 63).astype(F32) + (REACH + 1)
    second_row = jnp.where(lane_g >= 64, 1.0, 0.0).astype(F32)

    def step(it, start, triples, unroll, last):
        grouped = []
        for comp in range(2):
            even = disp[it, comp, pl.ds(0, pairs, stride=2), :]
            odd = disp[it, comp, pl.ds(1, pairs, stride=2), :]
            grouped.append(jnp.concatenate(halves(even, odd, low_half), axis=0))
        for comp in range(2):
            nearest = jnp.floor(grouped[comp] + 0.5)
            f = grouped[comp] - nearest
            at_w = 6 * comp
            weights[at_w] = 0.5 * (0.5 - f) * (0.5 - f)
            weights[at_w + 1] = 0.75 - f * f
            weights[at_w + 2] = 0.5 * (0.5 + f) * (0.5 + f)
            weights[at_w + 3] = f - 0.5
            weights[at_w + 4] = -2.0 * f
            weights[at_w + 5] = 0.5 + f
            if comp == 0:
                weights[12] = nearest + REACH + second_row
            else:
                weights[13] = nearest + position

        place = lax.broadcasted_iota(jnp.int32, (128, 128), 0).astype(F32).astype(BF16)
        one_bf, zero_bf = jnp.ones((128, 128), BF16), jnp.zeros((128, 128), BF16)

        def sample(index, carry):
            half = index // triples
            triple = lax.rem(index, triples)
            first_group = half * pairs + start + triple * 3
            columns = []
            for j in range(2):
                target = weights[13, pl.ds(first_group + j, 1), :]
                for b in range(3):
                    hit = place == jnp.broadcast_to((target + (b - 1)).astype(BF16), (128, 128))
                    columns.append(jnp.where(hit, one_bf, zero_bf))
            onehot = jnp.concatenate(columns, axis=1)
            begin = (start - first_pair) * 16 + triple * 48
            window = lhs[half, pl.ds(pl.multiple_of(begin, 16), 304), :]
            picked = dot(window, jnp.concatenate([onehot, onehot], axis=0))
            target = weights[13, pl.ds(first_group + 2, 1), :]
            lane_of = [
                jnp.broadcast_to((target + (b - 1)).astype(jnp.int32), (8, 128)) for b in range(3)
            ]

            def column_tap(j, k, b):
                if j < 2:
                    n = 3 * j + b
                    return picked[(2 * j + k) * 8 : (2 * j + k) * 8 + 8, n * 128 : n * 128 + 128]
                row = lhs_f32[half, pl.ds(pl.multiple_of(begin + 32 + k * 8, 8), 8), :]
                return jnp.take_along_axis(row, lane_of[b], axis=1, mode="promise_in_bounds")

            for j in range(3):
                group = first_group + j

                def weight(k):
                    return jnp.broadcast_to(weights[k, pl.ds(group, 1), :], (8, 128))

                offset = weight(12)
                masks = []
                for shift in (17, 8, 4, 2, 1, 1):
                    mask = offset >= shift
                    masks.append(mask)
                    offset = jnp.where(mask, offset - shift, offset)
                taps_at = []
                for b in range(3):
                    rows = [column_tap(j, k, b) for k in range(36)]
                    for shift, mask, count in zip(
                        (17, 8, 4, 2, 1, 1), masks, (19, 11, 7, 5, 4, 3)
                    ):
                        rows = [jnp.where(mask, rows[k + shift], rows[k]) for k in range(count)]
                    taps_at.append(rows)
                warped = slope_row = slope_col = None
                w_row, dw_row = [weight(a) for a in range(3)], [weight(3 + a) for a in range(3)]
                for b in range(3):
                    along = sum(w_row[a] * taps_at[b][a] for a in range(3))
                    slant = sum(dw_row[a] * taps_at[b][a] for a in range(3))
                    w, dw = weight(6 + b), weight(9 + b)
                    terms = (w * along, w * slant, dw * along)
                    if b == 0:
                        warped, slope_row, slope_col = terms
                    else:
                        warped += terms[0]
                        slope_row += terms[1]
                        slope_col += terms[2]
                mismatch = warped - fixed_embed[group]
                at_group = pl.ds(pl.multiple_of(group * CH, CH), CH)
                products[0, at_group, :] = mismatch * slope_row
                products[1, at_group, :] = mismatch * slope_col
            return carry

        lax.fori_loop(0, 2 * triples, sample, 0, unroll=unroll)

        for side in range(2):

            @pl.when(present(WEST_EAST[side]))
            def _():
                disp_copy(it, side).wait_recv()

        lane = lanes((ext_rows, tile_cols))
        one = jnp.where(it == 0, 1 / (1 - 0.9), jnp.where(it == 1, 1 / (1 - 0.9**2), 1 / (1 - 0.9**3)))
        two = jnp.where(
            it == 0, 1 / (1 - 0.999), jnp.where(it == 1, 1 / (1 - 0.999**2), 1 / (1 - 0.999**3))
        )
        for comp in range(2):
            summed = sum(products[comp, pl.ds(ch, 2 * pairs, stride=CH), :] for ch in range(CH))
            even, odd = halves(summed[0:pairs], summed[pairs : 2 * pairs], low_half)
            unpaired[comp, pl.ds(0, pairs, stride=2), :] = even
            unpaired[comp, pl.ds(1, pairs, stride=2), :] = odd
            sampled = unpaired[comp] * (2.0 / CH)
            d = disp[it, comp]
            north = pltpu.roll(d, 1, 0)
            south = pltpu.roll(d, ext_rows - 1, 0)
            from_west, from_east = edge_col[it, 0, 8:16, :], edge_col[it, 1, 0:8, :]
            tiles = range(comp * blocks, comp * blocks + blocks)
            west_in = [pltpu.roll(from_west, 128 - n, 1) if n else from_west for n in tiles]
            east_in = [pltpu.roll(from_east, 127 - n, 1) for n in tiles]
            west = jnp.where(lane == 0, jnp.concatenate(west_in, axis=0), pltpu.roll(d, 1, 1))
            east = jnp.where(
                lane == tile_cols - 1,
                jnp.concatenate(east_in, axis=0),
                pltpu.roll(d, tile_cols - 1, 1),
            )
            squashed = d * (1.0 / REACH)
            gradient = (
                sampled + 2.0 * stiffness * (4.0 * d - (south + north + east + west))
            ) * (1.0 - squashed * squashed)
            m1 = 0.9 * first_moment[comp] + 0.1 * gradient
            m2 = 0.999 * second_moment[comp] + 0.001 * gradient * gradient
            first_moment[comp] = m1
            second_moment[comp] = m2
            new = raw[comp] - step_size * (m1 * one) / (jnp.sqrt(m2 * two) + adam_epsilon)
            raw[comp] = new

            if not last:
                disp[it + 1, comp] = jnp.where(in_section, REACH * jnp.tanh(new / REACH), 0.0)

        if not last:
            send_disp(it + 1)

    def early(it, carry):
        step(it, first_pair, (tile_rows + 2 * EXTRA) // 6, 12, False)
        return carry

    lax.fori_loop(0, ITERS - 1, early, 0)
    step(ITERS - 1, first_pair, (tile_rows + 2 * EXTRA) // 6, 12, True)
    own_rows = slice(HALO, HALO + tile_rows)
    out_ref[...] = raw[:, own_rows, :] - field_ref[:, own_rows, :]
    for i, j in AROUND:

        @pl.when(present((-i, -j)))
        def _():
            for copy in image_copies(3 * (i + 1) + j + 1):
                copy.wait_send()

    for side in range(2):

        @pl.when(present(NORTH_SOUTH[1 - side]))
        def _():
            field_copy(side).wait_send()

        @pl.when(present(WEST_EAST[1 - side]))
        def _():
            for it in range(ITERS):
                disp_copy(it, side).wait_send()


def local(rows_of_mesh, cols_of_mesh, fixed, moving, field, w1, b1, w2):
    tile_rows, tile_cols = fixed.shape
    vmem = pl.BlockSpec(memory_space=pltpu.VMEM)
    tile = (tile_rows, tile_cols)
    ext = tile_rows + 2 * HALO
    return pl.pallas_call(
        functools.partial(kernel, rows_of_mesh, cols_of_mesh),
        out_shape=jax.ShapeDtypeStruct(field.shape, F32),
        in_specs=[pl.BlockSpec(memory_space=pltpu.HBM)] * 6,
        out_specs=vmem,
        scratch_shapes=[
            pltpu.VMEM((2, ext, tile_cols), F32),
            pltpu.VMEM(w1.shape, F32),
            pltpu.SMEM(b1.shape, F32),
            pltpu.VMEM(w2.shape, F32),
            pltpu.VMEM((2,) + tile, BF16),
            pltpu.VMEM((9, 2) + tile, BF16),
            pltpu.VMEM((3, 80, 256), F32),
            pltpu.VMEM((3 * SLAB * 8, 256), BF16),
            pltpu.VMEM((2, 70 * 8, 256), BF16),
            pltpu.VMEM((2, 70 * 8, 128), F32),
            pltpu.VMEM((ext, 8, 128), F32),
            pltpu.VMEM((ITERS, 2, ext, tile_cols), F32),
            pltpu.VMEM((ITERS, 16, 128), F32),
            pltpu.VMEM((ITERS, 2, 16, 128), F32),
            pltpu.VMEM((2, ext, tile_cols), F32),
            pltpu.VMEM((2, ext, tile_cols), F32),
            pltpu.VMEM((2, ext, tile_cols), F32),
            pltpu.VMEM((14, ext, 128), F32),
            pltpu.VMEM((2, ext * CH, 128), F32),
            pltpu.VMEM((2, ext, 128), F32),
            pltpu.SemaphoreType.DMA((1, 9)),
            pltpu.SemaphoreType.DMA((1, 9)),
            pltpu.SemaphoreType.DMA((2,)),
            pltpu.SemaphoreType.DMA((2,)),
            pltpu.SemaphoreType.DMA((ITERS, 2)),
            pltpu.SemaphoreType.DMA((ITERS, 2)),
            pltpu.SemaphoreType.DMA((6,)),
        ],
        compiler_params=pltpu.CompilerParams(
            collective_id=0, has_side_effects=True, vmem_limit_bytes=32 << 20
        ),
        name="refine",
    )(*(pltpu.with_memory_space_constraint(x, pltpu.HBM) for x in (fixed, moving, field, w1, b1, w2)))


def solution(mesh):
    return jax.shard_map(
        functools.partial(local, mesh.shape["row"], mesh.shape["col"]),
        mesh=mesh,
        in_specs=(P("row", "col"), P("row", "col"), P(None, "row", "col"), P(), P(), P()),
        out_specs=P(None, "row", "col"),
        check_vma=False,
    )
```

```python
import functools

import jax
import jax.numpy as jnp
from jax import lax
from jax.experimental import pallas as pl
from jax.experimental.pallas import tpu as pltpu
from jax.sharding import PartitionSpec as P

REACH = 16
ITERS = 3
CH = 8

stiffness = 0.01
step_size = 0.5
adam_epsilon = 0.01

F32 = jnp.float32
BF16 = jnp.bfloat16
MESH = pl.DeviceIdType.MESH
AROUND = [(-1, -1), (-1, 1), (1, -1), (1, 1), (-1, 0), (1, 0), (0, -1), (0, 1)]
NORTH_SOUTH = [(-1, 0), (1, 0)]
WEST_EAST = [(0, -1), (0, 1)]
HALO = 8
EXTRA = 2
SLAB = 14


def lanes(shape):
    return lax.broadcasted_iota(jnp.int32, shape, len(shape) - 1)


def split(x):
    high = x.astype(BF16)
    return high, (x - high.astype(F32)).astype(BF16)


def dot(a, b):
    return lax.dot_general(a, b, (((1,), (0,)), ((), ())), preferred_element_type=F32)


def kernel(
    rows_of_mesh,
    cols_of_mesh,
    fixed_hbm,
    moving_hbm,
    field_hbm,
    w1_hbm,
    b1_hbm,
    w2_hbm,
    out_ref,
    field_ref,
    w1_ref,
    b1_ref,
    w2_ref,
    own,
    around,
    shifted,
    toeplitz,
    lhs,
    lhs_f32,
    fixed_embed,
    disp,
    edges,
    edge_col,
    raw,
    first_moment,
    second_moment,
    weights,
    products,
    unpaired,
    image_send,
    image_recv,
    field_send,
    field_recv,
    disp_send,
    disp_recv,
    load_sem,
):
    me_row, me_col = lax.axis_index("row"), lax.axis_index("col")
    tile_rows, tile_cols = fixed_hbm.shape
    ext_rows = tile_rows + 2 * HALO

    def at(offset):
        return me_row + offset[0], me_col + offset[1]

    def present(offset):
        row, col = at(offset)
        return (row >= 0) & (row < rows_of_mesh) & (col >= 0) & (col < cols_of_mesh)

    barrier = pltpu.get_barrier_semaphore()
    for offset in AROUND:

        @pl.when(present(offset))
        def _():
            pl.semaphore_signal(barrier, inc=1, device_id=at(offset), device_id_type=MESH)

    loads = [
        pltpu.make_async_copy(src, dst, load_sem.at[i])
        for i, (src, dst) in enumerate(
            [
                (field_hbm, field_ref.at[:, pl.ds(HALO, tile_rows), :]),
                (moving_hbm, own.at[1]),
                (fixed_hbm, own.at[0]),
                (w2_hbm, w2_ref),
                (w1_hbm, w1_ref),
                (b1_hbm, b1_ref),
            ]
        )
    ]
    for load in loads:
        load.start()
    for offset in AROUND:
        slot = 3 * (offset[0] + 1) + offset[1] + 1

        @pl.when(jnp.logical_not(present(offset)))
        def _():
            around[slot] = jnp.zeros(around.shape[1:], BF16)

    for side in range(2):

        @pl.when(jnp.logical_not(present(NORTH_SOUTH[side])))
        def _():
            at_row = side * (HALO + tile_rows)
            field_ref[:, at_row : at_row + HALO, :] = jnp.zeros((2, HALO, tile_cols), F32)

        @pl.when(jnp.logical_not(present(WEST_EAST[side])))
        def _():
            edge_col[:, side] = jnp.zeros((ITERS,) + edge_col.shape[2:], F32)

    products[...] = jnp.zeros_like(products)
    first_moment[...] = jnp.zeros_like(first_moment)
    second_moment[...] = jnp.zeros_like(second_moment)

    def image_copies(slot):
        i, j = 1 - slot // 3, 1 - slot % 3
        return [
            pltpu.make_async_remote_copy(
                src_ref=own,
                dst_ref=around.at[slot],
                send_sem=image_send.at[0, slot],
                recv_sem=image_recv.at[0, slot],
                device_id=at((i, j)),
                device_id_type=MESH,
            )
        ]

    def field_copy(side):
        i, _ = NORTH_SOUTH[side]
        return pltpu.make_async_remote_copy(
            src_ref=field_hbm.at[:, pl.ds((tile_rows - HALO) * (1 - side), HALO), :],
            dst_ref=field_ref.at[:, pl.ds((HALO + tile_rows) * side, HALO), :],
            send_sem=field_send.at[side],
            recv_sem=field_recv.at[side],
            device_id=at((-i, 0)),
            device_id_type=MESH,
        )

    def disp_copy(step, side):
        _, j = WEST_EAST[side]
        return pltpu.make_async_remote_copy(
            src_ref=edges.at[step],
            dst_ref=edge_col.at[step, side],
            send_sem=disp_send.at[step, side],
            recv_sem=disp_recv.at[step, side],
            device_id=at((0, -j)),
            device_id_type=MESH,
        )

    lane_edge = lanes((8, 128))
    blocks = ext_rows // 8

    def send_disp(step):
        first, last = jnp.zeros((8, 128), F32), jnp.zeros((8, 128), F32)
        for n in range(2 * blocks):
            at_row = n % blocks * 8
            block = disp[step, n // blocks, at_row : at_row + 8, :]
            first = jnp.where(lane_edge == n, pltpu.roll(block, n, 1) if n else block, first)
            last = jnp.where(lane_edge == n, pltpu.roll(block, n + 1, 1), last)
        edges[step, 0:8, :] = first
        edges[step, 8:16, :] = last
        for side in range(2):

            @pl.when(present(WEST_EAST[1 - side]))
            def _():
                disp_copy(step, side).start()

    for load in loads:
        load.wait()

    rows_near = 1 + (me_row > 0).astype(jnp.int32) + (me_row < rows_of_mesh - 1).astype(jnp.int32)
    cols_near = 1 + (me_col > 0).astype(jnp.int32) + (me_col < cols_of_mesh - 1).astype(jnp.int32)
    pl.semaphore_wait(barrier, rows_near * cols_near - 1)
    for i, j in AROUND:

        @pl.when(present((-i, -j)))
        def _():
            for copy in image_copies(3 * (i + 1) + j + 1):
                copy.start()

    for side in range(2):

        @pl.when(present(NORTH_SOUTH[1 - side]))
        def _():
            field_copy(side).start()

    sub64 = lax.broadcasted_iota(jnp.int32, (64, 128), 0)
    lane64 = lanes((64, 128))
    w2 = w2_ref[...].reshape(64, 9)
    for tap_col in range(3):
        spread = jnp.zeros((64, 128), F32)
        for tap_row in range(3):
            column = w2[:, 3 * tap_row + tap_col : 3 * tap_row + tap_col + 1]
            spread = jnp.where(
                lane64 == tap_row * 8 + (sub64 & 7), jnp.broadcast_to(column, (64, 128)), spread
            )
        base = jnp.sum(spread.reshape(8, 8, 128), axis=1)
        block = jnp.concatenate(
            [base if i == 0 else pltpu.roll(base, 8 * i, 1) for i in range(SLAB)], axis=0
        )
        high, low = split(block)
        at_row = tap_col * SLAB * 8
        toeplitz[at_row : at_row + SLAB * 8, 0:128] = high
        toeplitz[at_row : at_row + SLAB * 8, 128:256] = low
    w1 = w1_ref[...]
    taps = [jnp.broadcast_to(w1[:, k : k + 1], (8, 256)) for k in range(9)]
    sub8 = lax.broadcasted_iota(jnp.int32, (8, 256), 0)
    bias = jnp.zeros((8, 256), F32)
    for ch in range(CH):
        bias = jnp.where(sub8 == ch, b1_ref[ch], bias)

    for side in range(2):

        @pl.when(present(NORTH_SOUTH[side]))
        def _():
            field_copy(side).wait_recv()

    full_rows, full_cols = rows_of_mesh * tile_rows, cols_of_mesh * tile_cols
    row_ext = me_row * tile_rows - HALO + lax.broadcasted_iota(
        jnp.int32, (ext_rows, tile_cols), 0
    )
    in_section = (row_ext >= 0) & (row_ext < full_rows)
    for comp in range(2):
        raw[comp] = field_ref[comp]
        disp[0, comp, 0:ext_rows, :] = jnp.where(in_section, REACH * jnp.tanh(field_ref[comp] / REACH), 0.0)
    send_disp(0)

    for i, j in AROUND:

        @pl.when(present((i, j)))
        def _():
            for copy in image_copies(3 * (i + 1) + j + 1):
                copy.wait_recv()

    lane_tile = lanes((80, 128))

    def encode(which, first_lane, first_row, row_margin, margin, slabs, store):
        def tile(slot):
            if slot == 4:
                return own[which].astype(F32)
            return around[slot, which].astype(F32)

        bands = []
        for col in range(3):
            bands.append(
                jnp.concatenate(
                    [tile(col)[8:, :], tile(3 + col), tile(6 + col)[: tile_rows - 8, :]], axis=0
                )
            )
        for tap_col in range(3):
            start = first_lane + tap_col
            if start == 128:
                left, right = bands[1], bands[2]
            else:
                turned = [pltpu.roll(x, 128 - start, 1) for x in bands]
                inside = lane_tile < 128 - start
                left = jnp.where(inside, turned[0], turned[1])
                right = jnp.where(inside, turned[1], turned[2])
            shifted[tap_col, :, 0:128] = left
            shifted[tap_col, :, 128:256] = right

        lane8 = lanes((8, 256))
        col8 = me_col * tile_cols + lane8 - (margin + 1)
        col_in = (col8 >= 0) & (col8 < full_cols)
        lane_e = lanes((SLAB * 8, 256))
        row_e = lax.broadcasted_iota(jnp.int32, (SLAB * 8, 256), 0) // 8
        col_e = me_col * tile_cols + lane_e - margin
        ok_col = (col_e >= 0) & (col_e < full_cols) & (lane_e < tile_cols + 2 * margin)

        for slab in slabs:
            hidden = []
            pixels = {}
            for i in range(SLAB + 4):
                for tap_col in range(3):
                    pixel = shifted[tap_col, pl.ds(first_row + slab + i, 1), :]
                    pixels[i, tap_col] = jnp.broadcast_to(pixel, (8, 256))
            for i in range(SLAB + 2):
                h = bias
                for tap in range(9):
                    h = h + taps[tap] * pixels[i + tap // 3, tap % 3]
                row = me_row * tile_rows + (slab + i - row_margin - 1)
                row_ok = (row >= 0) & (row < full_rows)
                row_factor = jnp.where(row_ok, 1.0, 0.0).astype(F32)
                hidden.append(jnp.where(col_in, jnp.maximum(h, 0.0) * row_factor, 0.0))
            high, low = split(jnp.concatenate(hidden, axis=0))
            t_high, t_low = toeplitz[:, 0:128], toeplitz[:, 128:256]
            product = dot(
                jnp.concatenate([t_high, t_high], axis=1), jnp.concatenate([high, low], axis=0)
            ) + dot(t_low, high)
            n = SLAB * 8
            embed = (
                product[0:n]
                + pltpu.roll(product[n : 2 * n], 255, 1)
                + pltpu.roll(product[2 * n : 3 * n], 254, 1)
            )
            row_abs = me_row * tile_rows + row_e + (slab - row_margin)
            embed = jnp.where(ok_col & (row_abs >= 0) & (row_abs < full_rows), embed, 0.0)
            store(slab, embed)

    def halves(even, odd, low_half):
        axis = even.ndim - 1
        return (
            jnp.where(low_half, even, pltpu.roll(odd, 64, axis)),
            jnp.where(low_half, pltpu.roll(even, 64, axis), odd),
        )

    low8 = lanes((8, 128)) < 64
    pairs = ext_rows // 2
    first_pair = (HALO - EXTRA) // 2

    def store_fixed(slab, embed):
        for pair in range(SLAB // 2):
            even = embed[pair * 16 : pair * 16 + 8, 0:128]
            odd = embed[pair * 16 + 8 : pair * 16 + 16, 0:128]
            left, right = halves(even, odd, low8)
            at_pair = first_pair + slab // 2 + pair
            fixed_embed[at_pair] = left
            fixed_embed[pairs + at_pair] = right

    low_e = lanes((SLAB * 8, 128)) < 64

    def store_moving(slab, embed):
        a, b = embed[:, 0:128], embed[:, 128:256]
        middle = jnp.where(low_e, pltpu.roll(a, 64, 1), pltpu.roll(b, 64, 1))
        for half, part in enumerate((a, middle)):
            lhs_f32[half, slab * 8 : (slab + SLAB) * 8, :] = part
            high, low = split(part)
            lhs[half, slab * 8 : (slab + SLAB) * 8, 0:128] = high
            lhs[half, slab * 8 : (slab + SLAB) * 8, 128:256] = low

    encode(0, 126, 24 - EXTRA - 2, EXTRA, 0, (0, 14, 22), store_fixed)
    encode(
        1, 109, 24 - EXTRA - REACH - 3, EXTRA + REACH + 1, REACH + 1, (0, 14, 28, 42, 56), store_moving
    )

    low_half = lanes((pairs, 128)) < 64
    lane_g = lanes((2 * pairs, 128))
    position = (lane_g & 63).astype(F32) + (REACH + 1)
    second_row = jnp.where(lane_g >= 64, 1.0, 0.0).astype(F32)

    def step(it, start, triples, unroll, last):
        grouped = []
        for comp in range(2):
            even = disp[it, comp, pl.ds(0, pairs, stride=2), :]
            odd = disp[it, comp, pl.ds(1, pairs, stride=2), :]
            grouped.append(jnp.concatenate(halves(even, odd, low_half), axis=0))
        for comp in range(2):
            nearest = jnp.floor(grouped[comp] + 0.5)
            f = grouped[comp] - nearest
            at_w = 6 * comp
            weights[at_w] = 0.5 * (0.5 - f) * (0.5 - f)
            weights[at_w + 1] = 0.75 - f * f
            weights[at_w + 2] = 0.5 * (0.5 + f) * (0.5 + f)
            weights[at_w + 3] = f - 0.5
            weights[at_w + 4] = -2.0 * f
            weights[at_w + 5] = 0.5 + f
            if comp == 0:
                weights[12] = nearest + REACH + second_row
            else:
                weights[13] = nearest + position

        place = lax.broadcasted_iota(jnp.int32, (128, 128), 0).astype(F32).astype(BF16)
        one_bf, zero_bf = jnp.ones((128, 128), BF16), jnp.zeros((128, 128), BF16)

        def sample(index, carry):
            half = index // triples
            triple = lax.rem(index, triples)
            first_group = half * pairs + start + triple * 3
            columns = []
            for j in range(2):
                target = weights[13, pl.ds(first_group + j, 1), :]
                for b in range(3):
                    hit = place == jnp.broadcast_to((target + (b - 1)).astype(BF16), (128, 128))
                    columns.append(jnp.where(hit, one_bf, zero_bf))
            onehot = jnp.concatenate(columns, axis=1)
            begin = (start - first_pair) * 16 + triple * 48
            window = lhs[half, pl.ds(pl.multiple_of(begin, 16), 304), :]
            picked = dot(window, jnp.concatenate([onehot, onehot], axis=0))
            target = weights[13, pl.ds(first_group + 2, 1), :]
            lane_of = [
                jnp.broadcast_to((target + (b - 1)).astype(jnp.int32), (8, 128)) for b in range(3)
            ]

            def column_tap(j, k, b):
                if j < 2:
                    n = 3 * j + b
                    return picked[(2 * j + k) * 8 : (2 * j + k) * 8 + 8, n * 128 : n * 128 + 128]
                row = lhs_f32[half, pl.ds(pl.multiple_of(begin + 32 + k * 8, 8), 8), :]
                return jnp.take_along_axis(row, lane_of[b], axis=1, mode="promise_in_bounds")

            for j in range(3):
                group = first_group + j

                def weight(k):
                    return jnp.broadcast_to(weights[k, pl.ds(group, 1), :], (8, 128))

                offset = weight(12)
                masks = []
                for shift in (17, 8, 4, 2, 1, 1):
                    mask = offset >= shift
                    masks.append(mask)
                    offset = jnp.where(mask, offset - shift, offset)
                taps_at = []
                for b in range(3):
                    rows = [column_tap(j, k, b) for k in range(36)]
                    for shift, mask, count in zip(
                        (17, 8, 4, 2, 1, 1), masks, (19, 11, 7, 5, 4, 3)
                    ):
                        rows = [jnp.where(mask, rows[k + shift], rows[k]) for k in range(count)]
                    taps_at.append(rows)
                warped = slope_row = slope_col = None
                w_row, dw_row = [weight(a) for a in range(3)], [weight(3 + a) for a in range(3)]
                for b in range(3):
                    along = sum(w_row[a] * taps_at[b][a] for a in range(3))
                    slant = sum(dw_row[a] * taps_at[b][a] for a in range(3))
                    w, dw = weight(6 + b), weight(9 + b)
                    terms = (w * along, w * slant, dw * along)
                    if b == 0:
                        warped, slope_row, slope_col = terms
                    else:
                        warped += terms[0]
                        slope_row += terms[1]
                        slope_col += terms[2]
                mismatch = warped - fixed_embed[group]
                at_group = pl.ds(pl.multiple_of(group * CH, CH), CH)
                products[0, at_group, :] = mismatch * slope_row
                products[1, at_group, :] = mismatch * slope_col
            return carry

        lax.fori_loop(0, 2 * triples, sample, 0, unroll=unroll)

        for side in range(2):

            @pl.when(present(WEST_EAST[side]))
            def _():
                disp_copy(it, side).wait_recv()

        lane = lanes((ext_rows, tile_cols))
        one = jnp.where(it == 0, 1 / (1 - 0.9), jnp.where(it == 1, 1 / (1 - 0.9**2), 1 / (1 - 0.9**3)))
        two = jnp.where(
            it == 0, 1 / (1 - 0.999), jnp.where(it == 1, 1 / (1 - 0.999**2), 1 / (1 - 0.999**3))
        )
        for comp in range(2):
            summed = sum(products[comp, pl.ds(ch, 2 * pairs, stride=CH), :] for ch in range(CH))
            even, odd = halves(summed[0:pairs], summed[pairs : 2 * pairs], low_half)
            unpaired[comp, pl.ds(0, pairs, stride=2), :] = even
            unpaired[comp, pl.ds(1, pairs, stride=2), :] = odd
            sampled = unpaired[comp, 0:ext_rows, :] * (2.0 / CH)
            d = disp[it, comp, 0:ext_rows, :]
            north = pltpu.roll(d, 1, 0)
            south = pltpu.roll(d, ext_rows - 1, 0)
            from_west, from_east = edge_col[it, 0, 8:16, :], edge_col[it, 1, 0:8, :]
            tiles = range(comp * blocks, comp * blocks + blocks)
            west_in = [pltpu.roll(from_west, 128 - n, 1) if n else from_west for n in tiles]
            east_in = [pltpu.roll(from_east, 127 - n, 1) for n in tiles]
            west = jnp.where(lane == 0, jnp.concatenate(west_in, axis=0), pltpu.roll(d, 1, 1))
            east = jnp.where(
                lane == tile_cols - 1,
                jnp.concatenate(east_in, axis=0),
                pltpu.roll(d, tile_cols - 1, 1),
            )
            squashed = d * (1.0 / REACH)
            gradient = (
                sampled + 2.0 * stiffness * (4.0 * d - (south + north + east + west))
            ) * (1.0 - squashed * squashed)
            m1 = 0.9 * first_moment[comp] + 0.1 * gradient
            m2 = 0.999 * second_moment[comp] + 0.001 * gradient * gradient
            first_moment[comp] = m1
            second_moment[comp] = m2
            new = raw[comp] - step_size * (m1 * one) / (jnp.sqrt(m2 * two) + adam_epsilon)
            raw[comp] = new

            if not last:
                disp[it + 1, comp, 0:ext_rows, :] = jnp.where(in_section, REACH * jnp.tanh(new / REACH), 0.0)

        if not last:
            send_disp(it + 1)

    def early(it, carry):
        step(it, first_pair, (tile_rows + 2 * EXTRA) // 6, 12, False)
        return carry

    lax.fori_loop(0, ITERS - 1, early, 0)
    step(ITERS - 1, first_pair, (tile_rows + 2 * EXTRA) // 6, 12, True)
    own_rows = slice(HALO, HALO + tile_rows)
    out_ref[...] = raw[:, own_rows, :] - field_ref[:, own_rows, :]
    for i, j in AROUND:

        @pl.when(present((-i, -j)))
        def _():
            for copy in image_copies(3 * (i + 1) + j + 1):
                copy.wait_send()

    for side in range(2):

        @pl.when(present(NORTH_SOUTH[1 - side]))
        def _():
            field_copy(side).wait_send()

        @pl.when(present(WEST_EAST[1 - side]))
        def _():
            for it in range(ITERS):
                disp_copy(it, side).wait_send()


def local(rows_of_mesh, cols_of_mesh, fixed, moving, field, w1, b1, w2):
    tile_rows, tile_cols = fixed.shape
    vmem = pl.BlockSpec(memory_space=pltpu.VMEM)
    tile = (tile_rows, tile_cols)
    ext = tile_rows + 2 * HALO
    return pl.pallas_call(
        functools.partial(kernel, rows_of_mesh, cols_of_mesh),
        out_shape=jax.ShapeDtypeStruct(field.shape, F32),
        in_specs=[pl.BlockSpec(memory_space=pltpu.HBM)] * 6,
        out_specs=vmem,
        scratch_shapes=[
            pltpu.VMEM((2, ext, tile_cols), F32),
            pltpu.VMEM(w1.shape, F32),
            pltpu.SMEM(b1.shape, F32),
            pltpu.VMEM(w2.shape, F32),
            pltpu.VMEM((2,) + tile, BF16),
            pltpu.VMEM((9, 2) + tile, BF16),
            pltpu.VMEM((3, 80, 256), F32),
            pltpu.VMEM((3 * SLAB * 8, 256), BF16),
            pltpu.VMEM((2, 70 * 8, 256), BF16),
            pltpu.VMEM((2, 70 * 8, 128), F32),
            pltpu.VMEM((ext, 8, 128), F32),
            pltpu.VMEM((ITERS, 2, ext + 8, tile_cols), F32),
            pltpu.VMEM((ITERS, 16, 128), F32),
            pltpu.VMEM((ITERS, 2, 16, 128), F32),
            pltpu.VMEM((2, ext, tile_cols), F32),
            pltpu.VMEM((2, ext, tile_cols), F32),
            pltpu.VMEM((2, ext, tile_cols), F32),
            pltpu.VMEM((14, ext, 128), F32),
            pltpu.VMEM((2, ext * CH + 8, 128), F32),
            pltpu.VMEM((2, ext + 8, 128), F32),
            pltpu.SemaphoreType.DMA((1, 9)),
            pltpu.SemaphoreType.DMA((1, 9)),
            pltpu.SemaphoreType.DMA((2,)),
            pltpu.SemaphoreType.DMA((2,)),
            pltpu.SemaphoreType.DMA((ITERS, 2)),
            pltpu.SemaphoreType.DMA((ITERS, 2)),
            pltpu.SemaphoreType.DMA((6,)),
        ],
        compiler_params=pltpu.CompilerParams(
            collective_id=0, has_side_effects=True, vmem_limit_bytes=32 << 20
        ),
        name="refine",
    )(*(pltpu.with_memory_space_constraint(x, pltpu.HBM) for x in (fixed, moving, field, w1, b1, w2)))


def solution(mesh):
    return jax.shard_map(
        functools.partial(local, mesh.shape["row"], mesh.shape["col"]),
        mesh=mesh,
        in_specs=(P("row", "col"), P("row", "col"), P(None, "row", "col"), P(), P(), P()),
        out_specs=P(None, "row", "col"),
        check_vma=False,
    )
```
